256 devices in a mesh: sx: 4 (over x_lo, core), sy: 8 (over z), ch: 8 (over x_hi, y).
Axes of the slice: x: 4 (x_hi: 2, x_lo: 2; x = x_hi * 2 + x_lo), y: 4, z: 8, core: 2. Of those that a mesh axis runs over, the one named last changes fastest.
Arguments:
- volume: bfloat16 [512, 32, 1024], P('ch', 'sx', 'sy'), may hold values from -6 to 6
- weight: bfloat16 [3, 3, 3, 512, 512], P(None, None, None, 'ch'), may hold values from -0.0546875 to 0.0546875
- bias: float32 [512], P('ch'), may hold values from -3 to 3
Outputs:
- convolved: bfloat16 [512, 32, 1024], P('ch', 'sx', 'sy')
The draws below stay inside these ranges and needn't reach their ends.
All inputs are finite; a program needn't handle non-finite values.
Results may differ from the reference program's by a relative error of at most 0.001.
Values may be sent and summed in bfloat16 or wider, within the bound.
A program may use at most 192 MiB of HBM per device.

```python
import jax
import jax.numpy as jnp
from jax import lax

C_IN = 512
C_OUT = 512
CZ = 16
NX = 32
NY = 64


def level_of(stream_key, shape, split, low, top_value):
    factor_of, own = 1.0, jax.random.fold_in(stream_key, 6)
    for axis_at, shards_of in split:
        heights = jnp.exp(jax.random.uniform(jax.random.fold_in(own, axis_at), (shards_of,), jnp.float32, low / len(split), top_value / len(split)))
        factor_of = factor_of * jnp.repeat(heights, shape[axis_at] // shards_of).reshape([-1 if axis == axis_at else 1 for axis in range(len(shape))])
    return factor_of


def bell_draw(rng, shape, spread, bound, split=(), held_as=jnp.bfloat16):
    values = jax.random.normal(rng, shape, jnp.float32) * spread
    if len(split) > 0:
        values = level_of(rng, shape, split, -0.22, 0.18) * values
    return jnp.clip(values, min=-bound, max=bound).astype(held_as)


def setup_inputs(seed: int = 0) -> dict:
    seeds = jax.random.split(jax.random.key(seed), 4)
    volume = bell_draw(seeds[0], (C_IN, NX, NY * CZ), 1.0, 6.0, ((0, 8), (1, 4), (2, 8)))
    weight = bell_draw(seeds[1], (3, 3, 3, C_OUT, C_IN), (27 * C_IN) ** -0.5, 0.0546875, ((3, 8),))
    bias = bell_draw(seeds[2], (C_OUT,), 0.5, 3.0, ((0, 8),), jnp.float32)
    return dict(volume=volume, weight=weight, bias=bias)


def reference(volume, weight, bias):
    cells = volume.reshape(C_IN, NX, NY, CZ).astype(jnp.float32)
    cells = jnp.transpose(cells, (1, 2, 3, 0))[None]
    filters = jnp.transpose(weight.astype(jnp.float32), (0, 1, 2, 4, 3))
    summed = lax.conv_general_dilated(
        cells,
        filters,
        (1, 1, 1),
        "SAME",
        dimension_numbers=("NDHWC", "DHWIO", "NDHWC"),
        precision=lax.Precision.HIGHEST,
        preferred_element_type=jnp.float32,
    )[0]
    summed = summed + bias.astype(jnp.float32)
    result = jnp.transpose(summed, (3, 0, 1, 2)).reshape(C_OUT, NX, NY * CZ)
    return result.astype(jnp.bfloat16)
```

```python
import jax
import jax.numpy as jnp
from jax import lax
from jax.experimental import pallas as pl
from jax.experimental.pallas import tpu as pltpu
from jax.sharding import PartitionSpec as P

CZ = 16
LANES = 128
MESH = pl.DeviceIdType.MESH
F32 = jnp.float32
BF16 = jnp.bfloat16


def kernel(sizes, v_hbm, w_hbm, b_ref, o_ref, X, W, V, acc, flat, hx, hy, hc, rx, ry, rc,
           load_sem, gs, gr, hs, hr):
    n_sx, n_sy, n_ch = sizes
    half_ch = n_ch // 2
    cin, cells_x = V.shape[0], V.shape[1]
    cout = W.shape[3]
    group = half_ch * cin
    sx, sy, ch = lax.axis_index("sx"), lax.axis_index("sy"), lax.axis_index("ch")
    h, y = ch // half_ch, lax.rem(ch, half_ch)

    def member(other, dy):
        return jnp.where(other == 1, 1 - h, h) * half_ch + lax.rem(y + dy, half_ch)

    def mate(other, dy):
        return (sx, sy, member(other, dy))

    def spatial(dx, dy):
        return (lax.rem(sx + dx + n_sx, n_sx), lax.rem(sy + dy + n_sy, n_sy), ch)

    load_v = pltpu.make_async_copy(v_hbm, V, load_sem.at[0])
    load_w = pltpu.make_async_copy(w_hbm, W, load_sem.at[1])
    load_v.start()
    load_w.start()

    barrier = pltpu.get_barrier_semaphore()
    mates = [(0, 1), (0, half_ch - 1), (0, 2), (1, 0)]
    spots = [(dx, dy) for dx in (-1, 0, 1) for dy in (-1, 0, 1) if (dx, dy) != (0, 0)]
    for m in mates:
        pl.semaphore_signal(barrier, inc=1, device_id=mate(*m), device_id_type=MESH)
    for s in spots:
        pl.semaphore_signal(barrier, inc=1, device_id=spatial(*s), device_id_type=MESH)

    lane = lax.broadcasted_iota(jnp.int32, (cin, LANES), 1)
    z = lax.rem(lane, CZ)

    load_v.wait()
    flat[...] = V[...].astype(F32).reshape(cin * cells_x, LANES)

    def rows(who):
        return pl.ds(pl.multiple_of(who * cin, cin), cin)

    zero = jnp.zeros((group * 2, LANES), BF16)
    for c in range(3):
        X[c, 0] = zero
        X[c, cells_x + 1] = zero

    mine = rows(ch)
    for x in range(cells_x):
        X[1, x + 1, mine, :] = flat[pl.ds(x, cin, stride=cells_x), :].astype(BF16)

    def shift_z(who):
        r = rows(who)
        for x in range(1, cells_x + 1):
            v = X[1, x, r, :]
            X[0, x, r, :] = jnp.where(z == 0, jnp.zeros_like(v), pltpu.roll(v, 1, 1))
            X[2, x, r, :] = jnp.where(z == CZ - 1, jnp.zeros_like(v), pltpu.roll(v, LANES - 1, 1))

    def send(who, slot, to):
        block = X.at[1, 1 : cells_x + 1, rows(who), :]
        copy = pltpu.make_async_remote_copy(
            src_ref=block, dst_ref=block, send_sem=gs.at[slot], recv_sem=gr.at[slot],
            device_id=to, device_id_type=MESH)
        copy.start()
        return copy

    def arrived(other, dy):
        slot = other * half_ch + dy
        block = X.at[1, 1 : cells_x + 1, rows(member(other, dy)), :]
        pltpu.make_async_remote_copy(
            src_ref=block, dst_ref=block, send_sem=gs.at[slot], recv_sem=gr.at[slot],
            device_id=mate(other, 0), device_id_type=MESH).wait_recv()

    pl.semaphore_wait(barrier, len(mates) + len(spots))
    sent = []
    sent.append(send(ch, half_ch + 0, mate(1, 0)))
    sent.append(send(ch, half_ch - 1, mate(0, 1)))
    sent.append(send(ch, 1, mate(0, half_ch - 1)))
    sent.append(send(ch, 2, mate(0, 2)))
    shift_z(ch)
    arrived(1, 0)
    sent.append(send(member(1, 0), half_ch + half_ch - 1, mate(0, 1)))
    sent.append(send(member(1, 0), half_ch + 1, mate(0, half_ch - 1)))
    shift_z(member(1, 0))
    arrived(0, 1)
    shift_z(member(0, 1))
    arrived(0, half_ch - 1)
    shift_z(member(0, half_ch - 1))
    arrived(0, 2)
    sent.append(send(member(0, 2), half_ch + 2, mate(1, 0)))
    shift_z(member(0, 2))
    load_w.wait()

    def products(which, first):
        cols = pl.ds(pl.multiple_of(which * group, group), group)
        for p in range((cells_x + 2) // 2):
            taps = [a for a in range(3) if 0 < 2 * p + a and 2 * p + a - 1 < cells_x + 1]
            lhs = jnp.concatenate(
                [W[a, :, c, :, cols].reshape(3 * cout, group) for a in taps for c in range(3)], axis=1)
            rhs = jnp.concatenate(
                [jnp.concatenate([X[c, 2 * p + a - 1, cols, :], X[c, 2 * p + a, cols, :]], axis=1)
                 for a in taps for c in range(3)], axis=0)
            r = jnp.dot(lhs, rhs, preferred_element_type=F32)
            for j in range(2):
                part = r[:, LANES * j : LANES * (j + 1)]
                if first:
                    acc[2 * p + j] = part
                else:
                    acc[2 * p + j] = acc[2 * p + j] + part

    products(h, True)
    arrived(1, 1)
    shift_z(member(1, 1))
    arrived(1, half_ch - 1)
    shift_z(member(1, half_ch - 1))
    arrived(1, 2)
    shift_z(member(1, 2))
    products(1 - h, False)

    lane_o = lax.broadcasted_iota(jnp.int32, (cout, LANES), 1)
    last = LANES - CZ

    def taps_of(s, b):
        return acc[s, b * cout : (b + 1) * cout]

    def along_y(s):
        up = jnp.where(lane_o < CZ, 0.0, pltpu.roll(taps_of(s, 0), CZ, 1))
        down = jnp.where(lane_o >= last, 0.0, pltpu.roll(taps_of(s, 2), LANES - CZ, 1))
        return taps_of(s, 1) + up + down

    def roll(v, by):
        by = by % LANES
        return pltpu.roll(v, by, 1) if by else v

    hx[0] = along_y(0)
    hx[1] = along_y(cells_x + 1)
    low = jnp.zeros((cout, LANES), F32)
    high = jnp.zeros((cout, LANES), F32)
    for x in range(cells_x):
        here = (lane_o >= x * CZ) & (lane_o < (x + 1) * CZ)
        low = jnp.where(here, roll(taps_of(x + 1, 2), x * CZ), low)
        high = jnp.where(here, roll(taps_of(x + 1, 0), x * CZ - last), high)
    hy[0] = low
    hy[1] = high
    rows_of = cout // 8
    lane_8 = lax.broadcasted_iota(jnp.int32, (8, LANES), 1)
    for i, s in enumerate((0, cells_x + 1)):
        for j, (b, start) in enumerate(((2, 0), (0, last))):
            corner = jnp.zeros((8, LANES), F32)
            for g in range(rows_of):
                here = (lane_8 >= g * CZ) & (lane_8 < (g + 1) * CZ)
                piece = acc[s, b * cout + 8 * g : b * cout + 8 * g + 8]
                corner = jnp.where(here, roll(piece, g * CZ - start), corner)
            hc[2 * i + j] = corner

    def give(src, dst, slot, to):
        copy = pltpu.make_async_remote_copy(
            src_ref=src, dst_ref=dst, send_sem=hs.at[slot], recv_sem=hr.at[slot],
            device_id=to, device_id_type=MESH)
        copy.start()
        return copy

    halos = []
    for i, d in enumerate((-1, 1)):
        halos.append(give(hy.at[i], ry.at[i], 2 + i, spatial(0, d)))
    for i, d in enumerate((-1, 1)):
        halos.append(give(hx.at[i], rx.at[i], i, spatial(d, 0)))
    for i, dx in enumerate((-1, 1)):
        for j, dy in enumerate((-1, 1)):
            k = 2 * i + j
            halos.append(give(hc.at[k], rc.at[k], 4 + k, spatial(dx, dy)))

    sub = lax.broadcasted_iota(jnp.int32, (cout, cout), 0)
    across = lax.broadcasted_iota(jnp.int32, (cout, cout), 1)
    bias = jnp.sum(jnp.where(sub == across, jnp.broadcast_to(b_ref[...], (cout, cout)), 0.0),
                   axis=1, keepdims=True)
    for x in range(cells_x):
        flat[pl.ds(x, cout, stride=cells_x), :] = along_y(x + 1) + bias

    for copy in halos:
        copy.wait()
    has = (sx > 0, sx < n_sx - 1)
    has_y = (sy > 0, sy < n_sy - 1)
    zeros = jnp.zeros((cout, LANES), F32)
    from_low_y = jnp.where(has_y[0], ry[1], zeros)
    from_high_y = jnp.where(has_y[1], ry[0], zeros)
    for x in range(cells_x):
        extra = jnp.where(lane_o < CZ, roll(from_low_y, -x * CZ), 0.0)
        extra = jnp.where(lane_o >= last, roll(from_high_y, last - x * CZ), extra)
        if x in (0, cells_x - 1):
            i = 0 if x == 0 else 1
            extra = extra + jnp.where(has[i], rx[1 - i], zeros)
            corners = []
            for j in range(2):
                start = 0 if j == 0 else last
                packed = jnp.where(has[i] & has_y[j], rc[2 * (1 - i) + 1 - j], jnp.zeros((8, LANES), F32))
                spread = jnp.concatenate([roll(packed, start - g * CZ) for g in range(rows_of)], axis=0)
                inside = lane_o < CZ if j == 0 else lane_o >= last
                extra = extra + jnp.where(inside, spread, 0.0)
        spot = pl.ds(x, cout, stride=cells_x)
        flat[spot, :] = flat[spot, :] + extra
    o_ref[...] = flat[...].reshape(cout, cells_x, LANES).astype(BF16)
    for copy in sent:
        copy.wait_send()


def solution(mesh):
    sizes = tuple(mesh.shape[a] for a in ("sx", "sy", "ch"))
    n_ch = sizes[2]

    def per_device(volume, weight, bias):
        cin, cells_x, merged = volume.shape
        cout = weight.shape[3]
        call = pl.pallas_call(
            lambda *refs: kernel(sizes, *refs),
            out_shape=jax.ShapeDtypeStruct((cout, cells_x, merged), BF16),
            in_specs=[
                pl.BlockSpec(memory_space=pl.ANY),
                pl.BlockSpec(memory_space=pl.ANY),
                pl.BlockSpec(memory_space=pltpu.VMEM),
            ],
            out_specs=pl.BlockSpec(memory_space=pltpu.VMEM),
            scratch_shapes=[
                pltpu.VMEM((3, cells_x + 2, n_ch * cin, LANES), BF16),
                pltpu.VMEM(weight.shape, BF16),
                pltpu.VMEM((cin, cells_x, LANES), BF16),
                pltpu.VMEM((cells_x + 2, 3 * cout, LANES), F32),
                pltpu.VMEM((cout * cells_x, LANES), F32),
                pltpu.VMEM((2, cout, LANES), F32),
                pltpu.VMEM((2, cout, LANES), F32),
                pltpu.VMEM((4, 8, LANES), F32),
                pltpu.VMEM((2, cout, LANES), F32),
                pltpu.VMEM((2, cout, LANES), F32),
                pltpu.VMEM((4, 8, LANES), F32),
                pltpu.SemaphoreType.DMA((2,)),
                pltpu.SemaphoreType.DMA((n_ch,)),
                pltpu.SemaphoreType.DMA((n_ch,)),
                pltpu.SemaphoreType.DMA((8,)),
                pltpu.SemaphoreType.DMA((8,)),
            ],
            compiler_params=pltpu.CompilerParams(
                collective_id=0, has_side_effects=True, vmem_limit_bytes=48 << 20),
            name="conv_gather",
        )
        return call(volume, weight, bias.reshape(1, cout))

    return jax.shard_map(
        per_device,
        mesh=mesh,
        in_specs=(P("ch", "sx", "sy"), P(None, None, None, "ch", None), P("ch")),
        out_specs=P("ch", "sx", "sy"),
        check_vma=False,
    )
```

```python
import jax
import jax.numpy as jnp
from jax import lax
from jax.experimental import pallas as pl
from jax.experimental.pallas import tpu as pltpu
from jax.sharding import PartitionSpec as P

CZ = 16
LANES = 128
MESH = pl.DeviceIdType.MESH
PARTS = 1
PLAN = [
    ("send", (0, 0), 0, (1, 0)),
    ("send", (0, 0), 0, (0, 1)),
    ("send", (0, 0), 0, (0, 3)),
    ("send", (0, 0), 0, (0, 2)),
    ("own",),
    ("wait", (1, 0), 0),
    ("send", (1, 0), 0, (0, 1)),
    ("send", (1, 0), 0, (0, 3)),
    ("wait", (0, 1), 0),
    ("wait", (0, 3), 0),
    ("wait", (0, 2), 0),
    ("send", (0, 2), 0, (1, 0)),
    ("first",),
    ("wait", (1, 1), 0),
    ("wait", (1, 3), 0),
    ("wait", (1, 2), 0),
    ("second",),
]
F32 = jnp.float32
BF16 = jnp.bfloat16


def kernel(sizes, v_hbm, w_hbm, b_hbm, o_ref, X, W, V, B, acc, flat, hx, hy, hc, rx, ry, rc,
           load_sem, gs, gr, hs, hr):
    n_sx, n_sy, n_ch = sizes
    half_ch = n_ch // 2
    cin, cells_x = V.shape[0], V.shape[1]
    cout = W.shape[3]
    group = half_ch * cin
    sx, sy, ch = lax.axis_index("sx"), lax.axis_index("sy"), lax.axis_index("ch")
    h, y = ch // half_ch, lax.rem(ch, half_ch)

    def member(other, k):
        across = (y, y + 1 - 2 * lax.rem(y, 2), lax.rem(y + 2, 4), 3 - y)[k]
        return (1 - h if other else h) * half_ch + across

    def mate(other, k):
        return (sx, sy, member(other, k))

    def spatial(dx, dy):
        return (sx + dx, sy + dy, ch)

    has_x = {-1: sx > 0, 0: sx >= 0, 1: sx < n_sx - 1}
    has_y = {-1: sy > 0, 0: sy >= 0, 1: sy < n_sy - 1}

    def exists(dx, dy):
        return has_x[dx] & has_y[dy]

    load_v = pltpu.make_async_copy(v_hbm, V, load_sem.at[0])
    load_w = pltpu.make_async_copy(w_hbm, W, load_sem.at[1])
    load_b = pltpu.make_async_copy(b_hbm, B, load_sem.at[2])
    load_v.start()
    load_b.start()
    load_w.start()

    barrier = pltpu.get_barrier_semaphore()
    mates = sorted({step[3] for step in PLAN if step[0] == "send"})
    spots = [(dx, dy) for dx in (-1, 0, 1) for dy in (-1, 0, 1) if (dx, dy) != (0, 0)]
    for m in mates:
        pl.semaphore_signal(barrier, inc=1, device_id=mate(*m), device_id_type=MESH)
    for s in spots:

        @pl.when(exists(*s))
        def _():
            pl.semaphore_signal(barrier, inc=1, device_id=spatial(*s), device_id_type=MESH)

    across_x = jnp.where(has_x[-1], 1, 0) + jnp.where(has_x[1], 1, 0) + 1
    across_y = jnp.where(has_y[-1], 1, 0) + jnp.where(has_y[1], 1, 0) + 1
    n_spots = across_x * across_y - 1

    lane = lax.broadcasted_iota(jnp.int32, (cin, LANES), 1)
    z = lax.rem(lane, CZ)

    load_v.wait()
    flat[...] = V[...].astype(F32).reshape(cin * cells_x, LANES)

    def rows(who):
        return pl.ds(pl.multiple_of(who * cin, cin), cin)

    zero = jnp.zeros((group * 2, LANES), BF16)
    for c in range(3):
        X[c, 0] = zero
        X[c, cells_x + 1] = zero

    mine = rows(ch)
    for x in range(cells_x):
        X[1, x + 1, mine, :] = flat[pl.ds(x, cin, stride=cells_x), :].astype(BF16)

    def shift_z(who, xs):
        r = rows(who)
        for x in xs:
            v = X[1, x + 1, r, :]
            X[0, x + 1, r, :] = jnp.where(z == 0, jnp.zeros_like(v), pltpu.roll(v, 1, 1))
            X[2, x + 1, r, :] = jnp.where(z == CZ - 1, jnp.zeros_like(v), pltpu.roll(v, LANES - 1, 1))

    def block_copy(block, part, out, slot, to):
        width = cells_x // PARTS
        piece = X.at[1, 1 + part * width : 1 + (part + 1) * width, rows(member(*block)), :]
        return pltpu.make_async_remote_copy(
            src_ref=piece, dst_ref=piece, send_sem=gs.at[out], recv_sem=gr.at[slot],
            device_id=mate(*to), device_id_type=MESH)

    sent = []

    def send(block, part, to):
        other, k = block[0] ^ to[0], block[1] ^ to[1]
        copy = block_copy(block, part, len(sent), (other * half_ch + k) * PARTS + part, to)
        copy.start()
        sent.append(copy)

    def arrived(block, part):
        block_copy(block, part, 0, (block[0] * half_ch + block[1]) * PARTS + part, (1, 0)).wait_recv()

    def products(which, first):
        cols = pl.ds(pl.multiple_of(which * group, group), group)
        for p in range((cells_x + 2) // 2):
            taps = [a for a in range(3) if 0 < 2 * p + a and 2 * p + a - 1 < cells_x + 1]
            lhs = jnp.concatenate(
                [W[a, :, c, :, cols].reshape(3 * cout, group) for a in taps for c in range(3)], axis=1)
            rhs = jnp.concatenate(
                [jnp.concatenate([X[c, 2 * p + a - 1, cols, :], X[c, 2 * p + a, cols, :]], axis=1)
                 for a in taps for c in range(3)], axis=0)
            r = jnp.dot(lhs, rhs, preferred_element_type=F32)
            for j in range(2):
                part = r[:, LANES * j : LANES * (j + 1)]
                if first:
                    acc[2 * p + j] = part
                else:
                    acc[2 * p + j] = acc[2 * p + j] + part

    pl.semaphore_wait(barrier, len(mates) + n_spots)
    for step in PLAN:
        if step[0] == "send":
            send(*step[1:])
        elif step[0] == "wait":
            arrived(*step[1:])
            width = cells_x // PARTS
            shift_z(member(*step[1]), range(step[2] * width, (step[2] + 1) * width))
        elif step[0] == "own":
            shift_z(ch, range(cells_x))
        elif step[0] == "first":
            load_w.wait()
            load_b.wait()
            products(h, True)
        else:
            products(1 - h, False)

    lane_o = lax.broadcasted_iota(jnp.int32, (cout, LANES), 1)
    last = LANES - CZ

    def taps_of(s, b):
        return acc[s, b * cout : (b + 1) * cout]

    def along_y(s):
        up = jnp.where(lane_o < CZ, 0.0, pltpu.roll(taps_of(s, 0), CZ, 1))
        down = jnp.where(lane_o >= last, 0.0, pltpu.roll(taps_of(s, 2), LANES - CZ, 1))
        return taps_of(s, 1) + up + down

    def roll(v, by):
        by = by % LANES
        return pltpu.roll(v, by, 1) if by else v

    hx[0] = along_y(0)
    hx[1] = along_y(cells_x + 1)
    low = jnp.zeros((cout, LANES), F32)
    high = jnp.zeros((cout, LANES), F32)
    for x in range(cells_x):
        here = (lane_o >= x * CZ) & (lane_o < (x + 1) * CZ)
        low = jnp.where(here, roll(taps_of(x + 1, 2), x * CZ), low)
        high = jnp.where(here, roll(taps_of(x + 1, 0), x * CZ - last), high)
    hy[0] = low
    hy[1] = high
    rows_of = cout // 8
    lane_8 = lax.broadcasted_iota(jnp.int32, (8, LANES), 1)
    for i, s in enumerate((0, cells_x + 1)):
        for j, (b, start) in enumerate(((2, 0), (0, last))):
            corner = jnp.zeros((8, LANES), F32)
            for g in range(rows_of):
                here = (lane_8 >= g * CZ) & (lane_8 < (g + 1) * CZ)
                piece = acc[s, b * cout + 8 * g : b * cout + 8 * g + 8]
                corner = jnp.where(here, roll(piece, g * CZ - start), corner)
            hc[2 * i + j] = corner

    edges = [(hy.at[0], ry.at[0], 0, -1), (hy.at[1], ry.at[1], 0, 1),
             (hx.at[0], rx.at[0], -1, 0), (hx.at[1], rx.at[1], 1, 0)]
    edges += [(hc.at[2 * i + j], rc.at[2 * i + j], dx, dy)
              for i, dx in enumerate((-1, 1)) for j, dy in enumerate((-1, 1))]

    def edge_copy(k):
        src, dst, dx, dy = edges[k]
        return pltpu.make_async_remote_copy(
            src_ref=src, dst_ref=dst, send_sem=hs.at[k], recv_sem=hr.at[k],
            device_id=spatial(dx, dy), device_id_type=MESH)

    for k, (_, _, dx, dy) in enumerate(edges):

        @pl.when(exists(dx, dy))
        def _():
            edge_copy(k).start()

    sub = lax.broadcasted_iota(jnp.int32, (cout, cout), 0)
    across = lax.broadcasted_iota(jnp.int32, (cout, cout), 1)
    bias = jnp.sum(jnp.where(sub == across, jnp.broadcast_to(B[...], (cout, cout)), 0.0),
                   axis=1, keepdims=True)
    for x in range(cells_x):
        flat[pl.ds(x, cout, stride=cells_x), :] = along_y(x + 1) + bias

    for k, (_, _, dx, dy) in enumerate(edges):

        @pl.when(exists(-dx, -dy))
        def _():
            edge_copy(k).wait_recv()

    has, has_end = (has_x[-1], has_x[1]), (has_y[-1], has_y[1])
    zeros = jnp.zeros((cout, LANES), F32)
    from_low_y = jnp.where(has_end[0], ry[1], zeros)
    from_high_y = jnp.where(has_end[1], ry[0], zeros)
    for x in range(cells_x):
        extra = jnp.where(lane_o < CZ, roll(from_low_y, -x * CZ), 0.0)
        extra = jnp.where(lane_o >= last, roll(from_high_y, last - x * CZ), extra)
        if x in (0, cells_x - 1):
            i = 0 if x == 0 else 1
            extra = extra + jnp.where(has[i], rx[1 - i], zeros)
            corners = []
            for j in range(2):
                start = 0 if j == 0 else last
                packed = jnp.where(has[i] & has_end[j], rc[2 * (1 - i) + 1 - j], jnp.zeros((8, LANES), F32))
                spread = jnp.concatenate([roll(packed, start - g * CZ) for g in range(rows_of)], axis=0)
                inside = lane_o < CZ if j == 0 else lane_o >= last
                extra = extra + jnp.where(inside, spread, 0.0)
        spot = pl.ds(x, cout, stride=cells_x)
        flat[spot, :] = flat[spot, :] + extra
    o_ref[...] = flat[...].reshape(cout, cells_x, LANES).astype(BF16)
    for k, (_, _, dx, dy) in enumerate(edges):

        @pl.when(exists(dx, dy))
        def _():
            edge_copy(k).wait_send()

    for copy in sent:
        copy.wait_send()


def solution(mesh):
    sizes = tuple(mesh.shape[a] for a in ("sx", "sy", "ch"))
    n_ch = sizes[2]

    def per_device(volume, weight, bias):
        cin, cells_x, merged = volume.shape
        cout = weight.shape[3]
        call = pl.pallas_call(
            lambda *refs: kernel(sizes, *refs),
            out_shape=pltpu.VMEM((cout, cells_x, merged), BF16),
            in_specs=[
                pl.BlockSpec(memory_space=pltpu.HBM),
                pl.BlockSpec(memory_space=pltpu.HBM),
                pl.BlockSpec(memory_space=pltpu.HBM),
            ],
            out_specs=pl.BlockSpec(memory_space=pltpu.VMEM),
            scratch_shapes=[
                pltpu.VMEM((3, cells_x + 2, n_ch * cin, LANES), BF16),
                pltpu.VMEM(weight.shape, BF16),
                pltpu.VMEM((cin, cells_x, LANES), BF16),
                pltpu.VMEM((1, cout), F32),
                pltpu.VMEM((cells_x + 2, 3 * cout, LANES), F32),
                pltpu.VMEM((cout * cells_x, LANES), F32),
                pltpu.VMEM((2, cout, LANES), F32),
                pltpu.VMEM((2, cout, LANES), F32),
                pltpu.VMEM((4, 8, LANES), F32),
                pltpu.VMEM((2, cout, LANES), F32),
                pltpu.VMEM((2, cout, LANES), F32),
                pltpu.VMEM((4, 8, LANES), F32),
                pltpu.SemaphoreType.DMA((3,)),
                pltpu.SemaphoreType.DMA((n_ch * PARTS,)),
                pltpu.SemaphoreType.DMA((n_ch * PARTS,)),
                pltpu.SemaphoreType.DMA((8,)),
                pltpu.SemaphoreType.DMA((8,)),
            ],
            compiler_params=pltpu.CompilerParams(
                collective_id=0, has_side_effects=True, vmem_limit_bytes=32 << 20),
            name="conv_gather",
        )
        return call(*[pltpu.with_memory_space_constraint(a, pltpu.HBM) for a in (volume, weight, bias.reshape(1, cout))])

    return jax.shard_map(
        per_device,
        mesh=mesh,
        in_specs=(P("ch", "sx", "sy"), P(None, None, None, "ch", None), P("ch")),
        out_specs=P("ch", "sx", "sy"),
        check_vma=False,
    )
```

```python
import jax
import jax.numpy as jnp
from jax import lax
from jax.experimental import pallas as pl
from jax.experimental.pallas import tpu as pltpu
from jax.sharding import PartitionSpec as P

CZ = 16
LANES = 128
MESH = pl.DeviceIdType.MESH
PARTS = 2
PLAN = [
    ('send', (0, 0), 0, (1, 0)),
    ('send', (0, 0), 1, (0, 1)),
    ('send', (0, 0), 0, (0, 3)),
    ('send', (0, 0), 1, (1, 0)),
    ('send', (0, 0), 0, (0, 1)),
    ('send', (0, 0), 1, (0, 3)),
    ('send', (0, 0), 0, (1, 2)),
    ('send', (0, 0), 1, (1, 2)),
    ('own',),
    ('wait', (0, 1), 1),
    ('send', (0, 1), 1, (0, 3)),
    ('send', (0, 1), 1, (1, 0)),
    ('wait', (0, 3), 0),
    ('send', (0, 3), 0, (0, 1)),
    ('send', (0, 3), 0, (1, 0)),
    ('wait', (1, 0), 0),
    ('send', (1, 0), 0, (0, 1)),
    ('wait', (1, 0), 1),
    ('send', (1, 0), 1, (0, 3)),
    ('wait', (0, 1), 0),
    ('wait', (0, 3), 1),
    ('wait', (0, 2), 0),
    ('wait', (0, 2), 1),
    ('first',),
    ('wait', (1, 1), 0),
    ('wait', (1, 3), 0),
    ('wait', (1, 1), 1),
    ('wait', (1, 3), 1),
    ('wait', (1, 2), 0),
    ('wait', (1, 2), 1),
    ('second',),
]
F32 = jnp.float32
BF16 = jnp.bfloat16


def kernel(sizes, v_hbm, w_hbm, b_hbm, o_ref, X, W, V, B, acc, flat, hx, hy, hc, rx, ry, rc,
           load_sem, gs, gr, hs, hr):
    n_sx, n_sy, n_ch = sizes
    half_ch = n_ch // 2
    cin, cells_x = V.shape[0], V.shape[1]
    cout = W.shape[3]
    group = half_ch * cin
    sx, sy, ch = lax.axis_index("sx"), lax.axis_index("sy"), lax.axis_index("ch")
    h, y = ch // half_ch, lax.rem(ch, half_ch)

    def member(other, k):
        across = (y, y + 1 - 2 * lax.rem(y, 2), lax.rem(y + 2, 4), 3 - y)[k]
        return (1 - h if other else h) * half_ch + across

    def mate(other, k):
        return (sx, sy, member(other, k))

    def spatial(dx, dy):
        return (sx + dx, sy + dy, ch)

    has_x = {-1: sx > 0, 0: sx >= 0, 1: sx < n_sx - 1}
    has_y = {-1: sy > 0, 0: sy >= 0, 1: sy < n_sy - 1}

    def exists(dx, dy):
        return has_x[dx] & has_y[dy]

    load_v = pltpu.make_async_copy(v_hbm, V, load_sem.at[0])
    load_w = pltpu.make_async_copy(w_hbm, W, load_sem.at[1])
    load_b = pltpu.make_async_copy(b_hbm, B, load_sem.at[2])
    load_v.start()
    load_b.start()
    load_w.start()

    barrier = pltpu.get_barrier_semaphore()
    mates = sorted({step[3] for step in PLAN if step[0] == "send"})
    spots = [(dx, dy) for dx in (-1, 0, 1) for dy in (-1, 0, 1) if (dx, dy) != (0, 0)]
    for m in mates:
        pl.semaphore_signal(barrier, inc=1, device_id=mate(*m), device_id_type=MESH)
    for s in spots:

        @pl.when(exists(*s))
        def _():
            pl.semaphore_signal(barrier, inc=1, device_id=spatial(*s), device_id_type=MESH)

    across_x = jnp.where(has_x[-1], 1, 0) + jnp.where(has_x[1], 1, 0) + 1
    across_y = jnp.where(has_y[-1], 1, 0) + jnp.where(has_y[1], 1, 0) + 1
    n_spots = across_x * across_y - 1

    lane = lax.broadcasted_iota(jnp.int32, (cin, LANES), 1)
    z = lax.rem(lane, CZ)

    load_v.wait()
    flat[...] = V[...].astype(F32).reshape(cin * cells_x, LANES)

    def rows(who):
        return pl.ds(pl.multiple_of(who * cin, cin), cin)

    zero = jnp.zeros((group * 2, LANES), BF16)
    for c in range(3):
        X[c, 0] = zero
        X[c, cells_x + 1] = zero

    mine = rows(ch)
    for x in range(cells_x):
        X[1, x + 1, mine, :] = flat[pl.ds(x, cin, stride=cells_x), :].astype(BF16)

    def shift_z(who, xs):
        r = rows(who)
        for x in xs:
            v = X[1, x + 1, r, :]
            X[0, x + 1, r, :] = jnp.where(z == 0, jnp.zeros_like(v), pltpu.roll(v, 1, 1))
            X[2, x + 1, r, :] = jnp.where(z == CZ - 1, jnp.zeros_like(v), pltpu.roll(v, LANES - 1, 1))

    def block_copy(block, part, out, slot, to):
        width = cells_x // PARTS
        piece = X.at[1, 1 + part * width : 1 + (part + 1) * width, rows(member(*block)), :]
        return pltpu.make_async_remote_copy(
            src_ref=piece, dst_ref=piece, send_sem=gs.at[out], recv_sem=gr.at[slot],
            device_id=mate(*to), device_id_type=MESH)

    sent = []

    def send(block, part, to):
        other, k = block[0] ^ to[0], block[1] ^ to[1]
        copy = block_copy(block, part, len(sent), (other * half_ch + k) * PARTS + part, to)
        copy.start()
        sent.append(copy)

    def arrived(block, part):
        block_copy(block, part, 0, (block[0] * half_ch + block[1]) * PARTS + part, (1, 0)).wait_recv()

    def products(which, first):
        cols = pl.ds(pl.multiple_of(which * group, group), group)
        for p in range((cells_x + 2) // 2):
            taps = [a for a in range(3) if 0 < 2 * p + a and 2 * p + a - 1 < cells_x + 1]
            lhs = jnp.concatenate(
                [W[a, :, c, :, cols].reshape(3 * cout, group) for a in taps for c in range(3)], axis=1)
            rhs = jnp.concatenate(
                [jnp.concatenate([X[c, 2 * p + a - 1, cols, :], X[c, 2 * p + a, cols, :]], axis=1)
                 for a in taps for c in range(3)], axis=0)
            r = jnp.dot(lhs, rhs, preferred_element_type=F32)
            for j in range(2):
                part = r[:, LANES * j : LANES * (j + 1)]
                if first:
                    acc[2 * p + j] = part
                else:
                    acc[2 * p + j] = acc[2 * p + j] + part

    pl.semaphore_wait(barrier, len(mates) + n_spots)
    for step in PLAN:
        if step[0] == "send":
            send(*step[1:])
        elif step[0] == "wait":
            arrived(*step[1:])
            width = cells_x // PARTS
            shift_z(member(*step[1]), range(step[2] * width, (step[2] + 1) * width))
        elif step[0] == "own":
            shift_z(ch, range(cells_x))
        elif step[0] == "first":
            load_w.wait()
            load_b.wait()
            products(h, True)
        else:
            products(1 - h, False)

    lane_o = lax.broadcasted_iota(jnp.int32, (cout, LANES), 1)
    last = LANES - CZ

    def taps_of(s, b):
        return acc[s, b * cout : (b + 1) * cout]

    def along_y(s):
        up = jnp.where(lane_o < CZ, 0.0, pltpu.roll(taps_of(s, 0), CZ, 1))
        down = jnp.where(lane_o >= last, 0.0, pltpu.roll(taps_of(s, 2), LANES - CZ, 1))
        return taps_of(s, 1) + up + down

    def roll(v, by):
        by = by % LANES
        return pltpu.roll(v, by, 1) if by else v

    hx[0] = along_y(0)
    hx[1] = along_y(cells_x + 1)
    low = jnp.zeros((cout, LANES), F32)
    high = jnp.zeros((cout, LANES), F32)
    for x in range(cells_x):
        here = (lane_o >= x * CZ) & (lane_o < (x + 1) * CZ)
        low = jnp.where(here, roll(taps_of(x + 1, 2), x * CZ), low)
        high = jnp.where(here, roll(taps_of(x + 1, 0), x * CZ - last), high)
    hy[0] = low
    hy[1] = high
    rows_of = cout // 8
    lane_8 = lax.broadcasted_iota(jnp.int32, (8, LANES), 1)
    for i, s in enumerate((0, cells_x + 1)):
        for j, (b, start) in enumerate(((2, 0), (0, last))):
            corner = jnp.zeros((8, LANES), F32)
            for g in range(rows_of):
                here = (lane_8 >= g * CZ) & (lane_8 < (g + 1) * CZ)
                piece = acc[s, b * cout + 8 * g : b * cout + 8 * g + 8]
                corner = jnp.where(here, roll(piece, g * CZ - start), corner)
            hc[2 * i + j] = corner

    edges = [(hy.at[0], ry.at[0], 0, -1), (hy.at[1], ry.at[1], 0, 1),
             (hx.at[0], rx.at[0], -1, 0), (hx.at[1], rx.at[1], 1, 0)]
    edges += [(hc.at[2 * i + j], rc.at[2 * i + j], dx, dy)
              for i, dx in enumerate((-1, 1)) for j, dy in enumerate((-1, 1))]

    def edge_copy(k):
        src, dst, dx, dy = edges[k]
        return pltpu.make_async_remote_copy(
            src_ref=src, dst_ref=dst, send_sem=hs.at[k], recv_sem=hr.at[k],
            device_id=spatial(dx, dy), device_id_type=MESH)

    for k, (_, _, dx, dy) in enumerate(edges):

        @pl.when(exists(dx, dy))
        def _():
            edge_copy(k).start()

    sub = lax.broadcasted_iota(jnp.int32, (cout, cout), 0)
    across = lax.broadcasted_iota(jnp.int32, (cout, cout), 1)
    bias = jnp.sum(jnp.where(sub == across, jnp.broadcast_to(B[...], (cout, cout)), 0.0),
                   axis=1, keepdims=True)
    for x in range(cells_x):
        flat[pl.ds(x, cout, stride=cells_x), :] = along_y(x + 1) + bias

    for k, (_, _, dx, dy) in enumerate(edges):

        @pl.when(exists(-dx, -dy))
        def _():
            edge_copy(k).wait_recv()

    has, has_end = (has_x[-1], has_x[1]), (has_y[-1], has_y[1])
    zeros = jnp.zeros((cout, LANES), F32)
    from_low_y = jnp.where(has_end[0], ry[1], zeros)
    from_high_y = jnp.where(has_end[1], ry[0], zeros)
    for x in range(cells_x):
        extra = jnp.where(lane_o < CZ, roll(from_low_y, -x * CZ), 0.0)
        extra = jnp.where(lane_o >= last, roll(from_high_y, last - x * CZ), extra)
        if x in (0, cells_x - 1):
            i = 0 if x == 0 else 1
            extra = extra + jnp.where(has[i], rx[1 - i], zeros)
            corners = []
            for j in range(2):
                start = 0 if j == 0 else last
                packed = jnp.where(has[i] & has_end[j], rc[2 * (1 - i) + 1 - j], jnp.zeros((8, LANES), F32))
                spread = jnp.concatenate([roll(packed, start - g * CZ) for g in range(rows_of)], axis=0)
                inside = lane_o < CZ if j == 0 else lane_o >= last
                extra = extra + jnp.where(inside, spread, 0.0)
        spot = pl.ds(x, cout, stride=cells_x)
        flat[spot, :] = flat[spot, :] + extra
    o_ref[...] = flat[...].reshape(cout, cells_x, LANES).astype(BF16)
    for k, (_, _, dx, dy) in enumerate(edges):

        @pl.when(exists(dx, dy))
        def _():
            edge_copy(k).wait_send()

    for copy in sent:
        copy.wait_send()


def solution(mesh):
    sizes = tuple(mesh.shape[a] for a in ("sx", "sy", "ch"))
    n_ch = sizes[2]

    def per_device(volume, weight, bias):
        cin, cells_x, merged = volume.shape
        cout = weight.shape[3]
        call = pl.pallas_call(
            lambda *refs: kernel(sizes, *refs),
            out_shape=pltpu.VMEM((cout, cells_x, merged), BF16),
            in_specs=[
                pl.BlockSpec(memory_space=pltpu.HBM),
                pl.BlockSpec(memory_space=pltpu.HBM),
                pl.BlockSpec(memory_space=pltpu.HBM),
            ],
            out_specs=pl.BlockSpec(memory_space=pltpu.VMEM),
            scratch_shapes=[
                pltpu.VMEM((3, cells_x + 2, n_ch * cin, LANES), BF16),
                pltpu.VMEM(weight.shape, BF16),
                pltpu.VMEM((cin, cells_x, LANES), BF16),
                pltpu.VMEM((1, cout), F32),
                pltpu.VMEM((cells_x + 2, 3 * cout, LANES), F32),
                pltpu.VMEM((cout * cells_x, LANES), F32),
                pltpu.VMEM((2, cout, LANES), F32),
                pltpu.VMEM((2, cout, LANES), F32),
                pltpu.VMEM((4, 8, LANES), F32),
                pltpu.VMEM((2, cout, LANES), F32),
                pltpu.VMEM((2, cout, LANES), F32),
                pltpu.VMEM((4, 8, LANES), F32),
                pltpu.SemaphoreType.DMA((3,)),
                pltpu.SemaphoreType.DMA((n_ch * PARTS,)),
                pltpu.SemaphoreType.DMA((n_ch * PARTS,)),
                pltpu.SemaphoreType.DMA((8,)),
                pltpu.SemaphoreType.DMA((8,)),
            ],
            compiler_params=pltpu.CompilerParams(
                collective_id=0, has_side_effects=True, vmem_limit_bytes=32 << 20),
            name="conv_gather",
        )
        return call(*[pltpu.with_memory_space_constraint(a, pltpu.HBM) for a in (volume, weight, bias.reshape(1, cout))])

    return jax.shard_map(
        per_device,
        mesh=mesh,
        in_specs=(P("ch", "sx", "sy"), P(None, None, None, "ch", None), P("ch")),
        out_specs=P("ch", "sx", "sy"),
        check_vma=False,
    )
```

```python
import jax
import jax.numpy as jnp
from jax import lax
from jax.experimental import pallas as pl
from jax.experimental.pallas import tpu as pltpu
from jax.sharding import PartitionSpec as P

CZ = 16
LANES = 128
MESH = pl.DeviceIdType.MESH
PARTS = 2
PLAN = [
    ('turn', 0),
    ('turn', 1),
    ('send', (0, 0), 0, (0, 2)),
    ('send', (0, 0), 0, (1, 0)),
    ('send', (0, 0), 1, (0, 2)),
    ('send', (0, 0), 1, (1, 0)),
    ('send', (0, 0), 1, (0, 1)),
    ('send', (0, 0), 0, (0, 3)),
    ('send', (0, 0), 0, (0, 1)),
    ('send', (0, 0), 1, (0, 3)),
    ('own',),
    ('wait', (0, 2), 0),
    ('send', (0, 2), 0, (1, 0)),
    ('wait', (1, 0), 0),
    ('send', (1, 0), 0, (0, 1)),
    ('send', (1, 0), 0, (0, 3)),
    ('wait', (0, 2), 1),
    ('send', (0, 2), 1, (1, 0)),
    ('wait', (1, 0), 1),
    ('send', (1, 0), 1, (0, 1)),
    ('send', (1, 0), 1, (0, 3)),
    ('wait', (0, 1), 0),
    ('wait', (0, 1), 1),
    ('first', (0, 0)),
    ('wait', (0, 3), 0),
    ('wait', (0, 3), 1),
    ('next', (0, 2)),
    ('wait', (1, 1), 0),
    ('wait', (1, 1), 1),
    ('next', (1, 0)),
    ('wait', (1, 3), 0),
    ('wait', (1, 3), 1),
    ('wait', (1, 2), 0),
    ('wait', (1, 2), 1),
    ('last', (1, 2)),
]
F32 = jnp.float32
BF16 = jnp.bfloat16


def kernel(sizes, v_hbm, w_hbm, b_hbm, o_ref, X, W, V, B, acc, flat, hx, hy, hc, rx, ry, rc,
           load_sem, gs, gr, hs, hr):
    n_sx, n_sy, n_ch = sizes
    half_ch = n_ch // 2
    cin, cells_x = V.shape[0], V.shape[1]
    cout = W.shape[3]
    group = half_ch * cin
    sx, sy, ch = lax.axis_index("sx"), lax.axis_index("sy"), lax.axis_index("ch")
    h, y = ch // half_ch, lax.rem(ch, half_ch)

    def member(other, k):
        across = (y, y + 1 - 2 * lax.rem(y, 2), lax.rem(y + 2, 4), 3 - y)[k]
        return (1 - h if other else h) * half_ch + across

    def mate(other, k):
        return (sx, sy, member(other, k))

    def spatial(dx, dy):
        return (sx + dx, sy + dy, ch)

    has_x = {-1: sx > 0, 0: sx >= 0, 1: sx < n_sx - 1}
    has_y = {-1: sy > 0, 0: sy >= 0, 1: sy < n_sy - 1}

    def exists(dx, dy):
        return has_x[dx] & has_y[dy]

    step_ch = cin // PARTS
    load_v = [pltpu.make_async_copy(v_hbm.at[pl.ds(p * step_ch, step_ch)], V.at[pl.ds(p * step_ch, step_ch)],
                                    load_sem.at[2 + p]) for p in range(PARTS)]
    load_w = pltpu.make_async_copy(w_hbm, W, load_sem.at[0])
    load_b = pltpu.make_async_copy(b_hbm, B, load_sem.at[1])
    for load in load_v:
        load.start()
    load_b.start()
    load_w.start()

    barrier = pltpu.get_barrier_semaphore()
    mates = sorted({step[3] for step in PLAN if step[0] == "send"})
    spots = [(dx, dy) for dx in (-1, 0, 1) for dy in (-1, 0, 1) if (dx, dy) != (0, 0)]
    for m in mates:
        pl.semaphore_signal(barrier, inc=1, device_id=mate(*m), device_id_type=MESH)
    for s in spots:

        @pl.when(exists(*s))
        def _():
            pl.semaphore_signal(barrier, inc=1, device_id=spatial(*s), device_id_type=MESH)

    across_x = jnp.where(has_x[-1], 1, 0) + jnp.where(has_x[1], 1, 0) + 1
    across_y = jnp.where(has_y[-1], 1, 0) + jnp.where(has_y[1], 1, 0) + 1
    n_spots = across_x * across_y - 1

    lane = lax.broadcasted_iota(jnp.int32, (step_ch, LANES), 1)
    z = lax.rem(lane, CZ)

    def rows(who, part):
        return pl.ds(pl.multiple_of(who * cin + part * step_ch, step_ch), step_ch)

    def turn(part):
        load_v[part].wait()
        n = step_ch * cells_x
        flat[part * n : (part + 1) * n] = V[pl.ds(part * step_ch, step_ch)].astype(F32).reshape(n, LANES)
        for x in range(cells_x):
            piece = flat[pl.ds(part * n + x, step_ch, stride=cells_x), :]
            X[1, x + 1, rows(ch, part), :] = piece.astype(BF16)

    def shift_z(who, part):
        r = rows(who, part)
        for x in range(1, cells_x + 1):
            v = X[1, x, r, :]
            X[0, x, r, :] = jnp.where(z == 0, jnp.zeros_like(v), pltpu.roll(v, 1, 1))
            X[2, x, r, :] = jnp.where(z == CZ - 1, jnp.zeros_like(v), pltpu.roll(v, LANES - 1, 1))

    def block_copy(block, part, out, slot, to):
        piece = X.at[1, 1 : cells_x + 1, rows(member(*block), part), :]
        return pltpu.make_async_remote_copy(
            src_ref=piece, dst_ref=piece, send_sem=gs.at[out], recv_sem=gr.at[slot],
            device_id=mate(*to), device_id_type=MESH)

    sent = []

    def send(block, part, to):
        other, k = block[0] ^ to[0], block[1] ^ to[1]
        copy = block_copy(block, part, len(sent), (other * half_ch + k) * PARTS + part, to)
        copy.start()
        sent.append(copy)

    def arrived(block, part):
        block_copy(block, part, 0, (block[0] * half_ch + block[1]) * PARTS + part, (1, 0)).wait_recv()

    pair = 2 * cin
    n_pairs = (cells_x + 2) // 2

    def products(block, first, rows_of, spans):
        cols = pl.ds(pl.multiple_of(member(*block) // 2 * pair, pair), pair)
        for p in spans:
            taps = [a for a in range(3) if 0 < 2 * p + a and 2 * p + a - 1 < cells_x + 1]
            lhs = jnp.concatenate(
                [jnp.concatenate([W[a, b, c, :, cols] for b in rows_of], axis=0) for a in taps for c in range(3)],
                axis=1)
            rhs = jnp.concatenate(
                [jnp.concatenate([X[c, 2 * p + a - 1, cols, :], X[c, 2 * p + a, cols, :]], axis=1)
                 for a in taps for c in range(3)], axis=0)
            r = jnp.dot(lhs, rhs, preferred_element_type=F32)
            for j in range(2):
                for i, b in enumerate(rows_of):
                    part = r[i * cout : (i + 1) * cout, LANES * j : LANES * (j + 1)]
                    spot = slice(b * cout, (b + 1) * cout)
                    acc[2 * p + j, spot] = part if first else acc[2 * p + j, spot] + part

    ready = False
    for step in PLAN:
        if step[0] == "turn":
            turn(step[1])
        elif step[0] == "send":
            if not ready:
                pl.semaphore_wait(barrier, len(mates) + n_spots)
                ready = True
            send(*step[1:])
        elif step[0] == "wait":
            arrived(*step[1:])
            shift_z(member(*step[1]), step[2])
        elif step[0] == "own":
            zero = jnp.zeros((n_ch * cin, LANES), BF16)
            for c in range(3):
                X[c, 0] = zero
                X[c, cells_x + 1] = zero
            for part in range(PARTS):
                shift_z(ch, part)
        elif step[0] == "first":
            load_w.wait()
            load_b.wait()
            products(step[1], True, (0, 1, 2), range(n_pairs))
        elif step[0] == "next":
            products(step[1], False, (0, 1, 2), range(n_pairs))
        else:
            products(step[1], False, (0, 1, 2), (0, n_pairs - 1))
            products(step[1], False, (0, 2), range(1, n_pairs - 1))

    lane_o = lax.broadcasted_iota(jnp.int32, (cout, LANES), 1)
    last = LANES - CZ

    def taps_of(s, b):
        return acc[s, b * cout : (b + 1) * cout]

    def along_y(s):
        up = jnp.where(lane_o < CZ, 0.0, pltpu.roll(taps_of(s, 0), CZ, 1))
        down = jnp.where(lane_o >= last, 0.0, pltpu.roll(taps_of(s, 2), LANES - CZ, 1))
        return taps_of(s, 1) + up + down

    def roll(v, by):
        by = by % LANES
        return pltpu.roll(v, by, 1) if by else v

    low = jnp.zeros((cout, LANES), F32)
    high = jnp.zeros((cout, LANES), F32)
    for x in range(cells_x):
        here = (lane_o >= x * CZ) & (lane_o < (x + 1) * CZ)
        low = jnp.where(here, roll(taps_of(x + 1, 2), x * CZ), low)
        high = jnp.where(here, roll(taps_of(x + 1, 0), x * CZ - last), high)
    hy[0] = low
    hy[1] = high
    edges = [(hy.at[0], ry.at[0], 0, -1), (hy.at[1], ry.at[1], 0, 1),
             (hx.at[0], rx.at[0], -1, 0), (hx.at[1], rx.at[1], 1, 0)]
    edges += [(hc.at[2 * i + j], rc.at[2 * i + j], dx, dy)
              for i, dx in enumerate((-1, 1)) for j, dy in enumerate((-1, 1))]

    def edge_copy(k):
        src, dst, dx, dy = edges[k]
        return pltpu.make_async_remote_copy(
            src_ref=src, dst_ref=dst, send_sem=hs.at[k], recv_sem=hr.at[k],
            device_id=spatial(dx, dy), device_id_type=MESH)

    def leave(ks):
        for k in ks:

            @pl.when(exists(*edges[k][2:]))
            def _():
                edge_copy(k).start()

    leave(range(2))
    groups = cout // 8
    lane_8 = lax.broadcasted_iota(jnp.int32, (8, LANES), 1)
    for i, s in enumerate((0, cells_x + 1)):
        for j, (b, start) in enumerate(((2, 0), (0, last))):
            corner = jnp.zeros((8, LANES), F32)
            for g in range(groups):
                here = (lane_8 >= g * CZ) & (lane_8 < (g + 1) * CZ)
                piece = acc[s, b * cout + 8 * g : b * cout + 8 * g + 8]
                corner = jnp.where(here, roll(piece, g * CZ - start), corner)
            hc[2 * i + j] = corner

    leave(range(4, 8))
    hx[0] = along_y(0)
    hx[1] = along_y(cells_x + 1)
    leave(range(2, 4))

    products(PLAN[-1][1], False, (1,), range(1, n_pairs - 1))
    sub = lax.broadcasted_iota(jnp.int32, (cout, cout), 0)
    across = lax.broadcasted_iota(jnp.int32, (cout, cout), 1)
    bias = jnp.sum(jnp.where(sub == across, jnp.broadcast_to(B[...], (cout, cout)), 0.0),
                   axis=1, keepdims=True)
    for x in range(cells_x):
        flat[pl.ds(x, cout, stride=cells_x), :] = along_y(x + 1) + bias

    for k, (_, _, dx, dy) in enumerate(edges):

        @pl.when(exists(-dx, -dy))
        def _():
            edge_copy(k).wait_recv()

    has, has_end = (has_x[-1], has_x[1]), (has_y[-1], has_y[1])
    zeros = jnp.zeros((cout, LANES), F32)
    from_low_y = jnp.where(has_end[0], ry[1], zeros)
    from_high_y = jnp.where(has_end[1], ry[0], zeros)
    for x in range(cells_x):
        extra = jnp.where(lane_o < CZ, roll(from_low_y, -x * CZ), 0.0)
        extra = jnp.where(lane_o >= last, roll(from_high_y, last - x * CZ), extra)
        if x in (0, cells_x - 1):
            i = 0 if x == 0 else 1
            extra = extra + jnp.where(has[i], rx[1 - i], zeros)
            corners = []
            for j in range(2):
                start = 0 if j == 0 else last
                packed = jnp.where(has[i] & has_end[j], rc[2 * (1 - i) + 1 - j], jnp.zeros((8, LANES), F32))
                spread = jnp.concatenate([roll(packed, start - g * CZ) for g in range(groups)], axis=0)
                inside = lane_o < CZ if j == 0 else lane_o >= last
                extra = extra + jnp.where(inside, spread, 0.0)
        spot = pl.ds(x, cout, stride=cells_x)
        flat[spot, :] = flat[spot, :] + extra
    o_ref[...] = flat[...].reshape(cout, cells_x, LANES).astype(BF16)
    for k, (_, _, dx, dy) in enumerate(edges):

        @pl.when(exists(dx, dy))
        def _():
            edge_copy(k).wait_send()

    for copy in sent:
        copy.wait_send()


def solution(mesh):
    sizes = tuple(mesh.shape[a] for a in ("sx", "sy", "ch"))
    n_ch = sizes[2]

    def per_device(volume, weight, bias):
        cin, cells_x, merged = volume.shape
        cout = weight.shape[3]
        call = pl.pallas_call(
            lambda *refs: kernel(sizes, *refs),
            out_shape=pltpu.VMEM((cout, cells_x, merged), BF16),
            in_specs=[
                pl.BlockSpec(memory_space=pltpu.HBM),
                pl.BlockSpec(memory_space=pltpu.HBM),
                pl.BlockSpec(memory_space=pltpu.HBM),
            ],
            out_specs=pl.BlockSpec(memory_space=pltpu.VMEM),
            scratch_shapes=[
                pltpu.VMEM((3, cells_x + 2, n_ch * cin, LANES), BF16),
                pltpu.VMEM(weight.shape, BF16),
                pltpu.VMEM((cin, cells_x, LANES), BF16),
                pltpu.VMEM((1, cout), F32),
                pltpu.VMEM((cells_x + 2, 3 * cout, LANES), F32),
                pltpu.VMEM((cout * cells_x, LANES), F32),
                pltpu.VMEM((2, cout, LANES), F32),
                pltpu.VMEM((2, cout, LANES), F32),
                pltpu.VMEM((4, 8, LANES), F32),
                pltpu.VMEM((2, cout, LANES), F32),
                pltpu.VMEM((2, cout, LANES), F32),
                pltpu.VMEM((4, 8, LANES), F32),
                pltpu.SemaphoreType.DMA((2 + PARTS,)),
                pltpu.SemaphoreType.DMA((n_ch * PARTS,)),
                pltpu.SemaphoreType.DMA((n_ch * PARTS,)),
                pltpu.SemaphoreType.DMA((8,)),
                pltpu.SemaphoreType.DMA((8,)),
            ],
            compiler_params=pltpu.CompilerParams(
                collective_id=0, has_side_effects=True, vmem_limit_bytes=32 << 20),
            name="conv_gather",
        )
        return call(*[pltpu.with_memory_space_constraint(a, pltpu.HBM) for a in (volume, weight, bias.reshape(1, cout))])

    return jax.shard_map(
        per_device,
        mesh=mesh,
        in_specs=(P("ch", "sx", "sy"), P(None, None, None, "ch", None), P("ch")),
        out_specs=P("ch", "sx", "sy"),
        check_vma=False,
    )
```

```python
import jax
import jax.numpy as jnp
from jax import lax
from jax.experimental import pallas as pl
from jax.experimental.pallas import tpu as pltpu
from jax.sharding import PartitionSpec as P

CZ = 16
LANES = 128
MESH = pl.DeviceIdType.MESH
PARTS = 2
PLAN = [
    ('turn', 0),
    ('turn', 1),
    ('send', (0, 0), 0, (1, 0)),
    ('send', (0, 0), 0, (0, 2)),
    ('send', (0, 0), 1, (1, 0)),
    ('send', (0, 0), 1, (0, 2)),
    ('send', (0, 0), 1, (0, 1)),
    ('send', (0, 0), 0, (0, 3)),
    ('send', (0, 0), 0, (0, 1)),
    ('send', (0, 0), 1, (0, 3)),
    ('own',),
    ('wait', (0, 2), 0),
    ('send', (0, 2), 0, (1, 0)),
    ('wait', (1, 0), 0),
    ('send', (1, 0), 0, (0, 1)),
    ('send', (1, 0), 0, (0, 3)),
    ('wait', (0, 2), 1),
    ('send', (0, 2), 1, (1, 0)),
    ('wait', (1, 0), 1),
    ('send', (1, 0), 1, (0, 1)),
    ('send', (1, 0), 1, (0, 3)),
    ('wait', (0, 1), 0),
    ('wait', (0, 1), 1),
    ('first', (0, 0)),
    ('wait', (0, 3), 0),
    ('wait', (0, 3), 1),
    ('next', (0, 2)),
    ('wait', (1, 1), 0),
    ('wait', (1, 1), 1),
    ('next', (1, 0)),
    ('wait', (1, 3), 0),
    ('wait', (1, 3), 1),
    ('wait', (1, 2), 0),
    ('wait', (1, 2), 1),
    ('last', (1, 2)),
]
F32 = jnp.float32
BF16 = jnp.bfloat16


def kernel(sizes, v_hbm, w_hbm, b_hbm, o_ref, X, W, V, B, acc, flat, hx, hy, hc, rx, ry, rc,
           load_sem, gs, gr, hs, hr, entered):
    n_sx, n_sy, n_ch = sizes
    half_ch = n_ch // 2
    cin, cells_x = V.shape[0], V.shape[1]
    cout = W.shape[3]
    group = half_ch * cin
    sx, sy, ch = lax.axis_index("sx"), lax.axis_index("sy"), lax.axis_index("ch")
    h, y = ch // half_ch, lax.rem(ch, half_ch)

    def member(other, k):
        across = (y, y + 1 - 2 * lax.rem(y, 2), lax.rem(y + 2, 4), 3 - y)[k]
        return (1 - h if other else h) * half_ch + across

    def mate(other, k):
        return (sx, sy, member(other, k))

    def spatial(dx, dy):
        return (sx + dx, sy + dy, ch)

    has_x = {-1: sx > 0, 0: sx >= 0, 1: sx < n_sx - 1}
    has_y = {-1: sy > 0, 0: sy >= 0, 1: sy < n_sy - 1}

    def exists(dx, dy):
        return has_x[dx] & has_y[dy]

    step_ch = cin // PARTS
    load_v = [pltpu.make_async_copy(v_hbm.at[pl.ds(p * step_ch, step_ch)], V.at[pl.ds(p * step_ch, step_ch)],
                                    load_sem.at[2 + p]) for p in range(PARTS)]
    load_w = pltpu.make_async_copy(w_hbm, W, load_sem.at[0])
    load_b = pltpu.make_async_copy(b_hbm, B, load_sem.at[1])
    for load in load_v:
        load.start()
    load_b.start()
    load_w.start()

    barrier = pltpu.get_barrier_semaphore()
    mates = sorted({step[3] for step in PLAN if step[0] == "send"})
    later = [(0, 1), (-1, 1), (1, 1), (1, 0)]
    earlier = [(-dx, -dy) for dx, dy in later]
    for m in mates:
        pl.semaphore_signal(barrier, inc=1, device_id=mate(*m), device_id_type=MESH)

    def tell(sem, places):
        for place in places:

            @pl.when(exists(*place))
            def _():
                pl.semaphore_signal(sem, inc=1, device_id=spatial(*place), device_id_type=MESH)

    def count(places):
        return sum(jnp.where(exists(*place), 1, 0) for place in places)

    tell(barrier, later)

    lane = lax.broadcasted_iota(jnp.int32, (step_ch, LANES), 1)
    z = lax.rem(lane, CZ)

    def rows(who, part):
        return pl.ds(pl.multiple_of(who * cin + part * step_ch, step_ch), step_ch)

    def turn(part):
        load_v[part].wait()
        n = step_ch * cells_x
        flat[part * n : (part + 1) * n] = V[pl.ds(part * step_ch, step_ch)].astype(F32).reshape(n, LANES)
        for x in range(cells_x):
            piece = flat[pl.ds(part * n + x, step_ch, stride=cells_x), :]
            X[1, x + 1, rows(ch, part), :] = piece.astype(BF16)

    def shift_z(who, part):
        r = rows(who, part)
        for x in range(1, cells_x + 1):
            v = X[1, x, r, :]
            X[0, x, r, :] = jnp.where(z == 0, jnp.zeros_like(v), pltpu.roll(v, 1, 1))
            X[2, x, r, :] = jnp.where(z == CZ - 1, jnp.zeros_like(v), pltpu.roll(v, LANES - 1, 1))

    def block_copy(block, part, out, slot, to):
        piece = X.at[1, 1 : cells_x + 1, rows(member(*block), part), :]
        return pltpu.make_async_remote_copy(
            src_ref=piece, dst_ref=piece, send_sem=gs.at[out], recv_sem=gr.at[slot],
            device_id=mate(*to), device_id_type=MESH)

    sent = []

    def send(block, part, to):
        other, k = block[0] ^ to[0], block[1] ^ to[1]
        copy = block_copy(block, part, len(sent), (other * half_ch + k) * PARTS + part, to)
        copy.start()
        sent.append(copy)

    def arrived(block, part):
        block_copy(block, part, 0, (block[0] * half_ch + block[1]) * PARTS + part, (1, 0)).wait_recv()

    pair = 2 * cin
    n_pairs = (cells_x + 2) // 2

    def products(block, first, rows_of, spans):
        cols = pl.ds(pl.multiple_of(member(*block) // 2 * pair, pair), pair)
        for p in spans:
            taps = [a for a in range(3) if 0 < 2 * p + a and 2 * p + a - 1 < cells_x + 1]
            lhs = jnp.concatenate(
                [jnp.concatenate([W[a, b, c, :, cols] for b in rows_of], axis=0) for a in taps for c in range(3)],
                axis=1)
            rhs = jnp.concatenate(
                [jnp.concatenate([X[c, 2 * p + a - 1, cols, :], X[c, 2 * p + a, cols, :]], axis=1)
                 for a in taps for c in range(3)], axis=0)
            r = jnp.dot(lhs, rhs, preferred_element_type=F32)
            for j in range(2):
                for i, b in enumerate(rows_of):
                    part = r[i * cout : (i + 1) * cout, LANES * j : LANES * (j + 1)]
                    spot = slice(b * cout, (b + 1) * cout)
                    acc[2 * p + j, spot] = part if first else acc[2 * p + j, spot] + part

    ready = False
    for step in PLAN:
        if step[0] == "turn":
            turn(step[1])
        elif step[0] == "send":
            if not ready:
                pl.semaphore_wait(barrier, len(mates) + count(earlier))
                ready = True
            send(*step[1:])
        elif step[0] == "wait":
            arrived(*step[1:])
            shift_z(member(*step[1]), step[2])
        elif step[0] == "own":
            tell(entered, earlier)
            zero = jnp.zeros((n_ch * cin, LANES), BF16)
            for c in range(3):
                X[c, 0] = zero
                X[c, cells_x + 1] = zero
            for part in range(PARTS):
                shift_z(ch, part)
        elif step[0] == "first":
            load_w.wait()
            load_b.wait()
            products(step[1], True, (0, 1, 2), range(n_pairs))
        elif step[0] == "next":
            products(step[1], False, (0, 1, 2), range(n_pairs))
        else:
            products(step[1], False, (0, 1, 2), (0, n_pairs - 1))
            products(step[1], False, (0, 2), range(1, n_pairs - 1))

    lane_o = lax.broadcasted_iota(jnp.int32, (cout, LANES), 1)
    last = LANES - CZ

    def taps_of(s, b):
        return acc[s, b * cout : (b + 1) * cout]

    def along_y(s):
        up = jnp.where(lane_o < CZ, 0.0, pltpu.roll(taps_of(s, 0), CZ, 1))
        down = jnp.where(lane_o >= last, 0.0, pltpu.roll(taps_of(s, 2), LANES - CZ, 1))
        return taps_of(s, 1) + up + down

    def roll(v, by):
        by = by % LANES
        return pltpu.roll(v, by, 1) if by else v

    low = jnp.zeros((cout, LANES), F32)
    high = jnp.zeros((cout, LANES), F32)
    for x in range(cells_x):
        here = (lane_o >= x * CZ) & (lane_o < (x + 1) * CZ)
        low = jnp.where(here, roll(taps_of(x + 1, 2), x * CZ), low)
        high = jnp.where(here, roll(taps_of(x + 1, 0), x * CZ - last), high)
    hy[0] = low
    hy[1] = high
    edges = [(hy.at[0], ry.at[0], 0, -1), (hy.at[1], ry.at[1], 0, 1),
             (hx.at[0], rx.at[0], -1, 0), (hx.at[1], rx.at[1], 1, 0)]
    edges += [(hc.at[2 * i + j], rc.at[2 * i + j], dx, dy)
              for i, dx in enumerate((-1, 1)) for j, dy in enumerate((-1, 1))]

    def edge_copy(k):
        src, dst, dx, dy = edges[k]
        return pltpu.make_async_remote_copy(
            src_ref=src, dst_ref=dst, send_sem=hs.at[k], recv_sem=hr.at[k],
            device_id=spatial(dx, dy), device_id_type=MESH)

    def leave(ks):
        for k in ks:

            @pl.when(exists(*edges[k][2:]))
            def _():
                edge_copy(k).start()

    some = count(later)

    @pl.when(some > 0)
    def _():
        pl.semaphore_wait(entered, some)

    leave(range(2))
    groups = cout // 8
    lane_8 = lax.broadcasted_iota(jnp.int32, (8, LANES), 1)
    for i, s in enumerate((0, cells_x + 1)):
        for j, (b, start) in enumerate(((2, 0), (0, last))):
            corner = jnp.zeros((8, LANES), F32)
            for g in range(groups):
                here = (lane_8 >= g * CZ) & (lane_8 < (g + 1) * CZ)
                piece = acc[s, b * cout + 8 * g : b * cout + 8 * g + 8]
                corner = jnp.where(here, roll(piece, g * CZ - start), corner)
            hc[2 * i + j] = corner

    leave(range(4, 8))
    hx[0] = along_y(0)
    hx[1] = along_y(cells_x + 1)
    leave(range(2, 4))

    products(PLAN[-1][1], False, (1,), range(1, n_pairs - 1))
    sub = lax.broadcasted_iota(jnp.int32, (cout, cout), 0)
    across = lax.broadcasted_iota(jnp.int32, (cout, cout), 1)
    bias = jnp.sum(jnp.where(sub == across, jnp.broadcast_to(B[...], (cout, cout)), 0.0),
                   axis=1, keepdims=True)
    for x in range(cells_x):
        flat[pl.ds(x, cout, stride=cells_x), :] = along_y(x + 1) + bias

    for k, (_, _, dx, dy) in enumerate(edges):

        @pl.when(exists(-dx, -dy))
        def _():
            edge_copy(k).wait_recv()

    has, has_end = (has_x[-1], has_x[1]), (has_y[-1], has_y[1])
    zeros = jnp.zeros((cout, LANES), F32)
    from_low_y = jnp.where(has_end[0], ry[1], zeros)
    from_high_y = jnp.where(has_end[1], ry[0], zeros)
    for x in range(cells_x):
        extra = jnp.where(lane_o < CZ, roll(from_low_y, -x * CZ), 0.0)
        extra = jnp.where(lane_o >= last, roll(from_high_y, last - x * CZ), extra)
        if x in (0, cells_x - 1):
            i = 0 if x == 0 else 1
            extra = extra + jnp.where(has[i], rx[1 - i], zeros)
            corners = []
            for j in range(2):
                start = 0 if j == 0 else last
                packed = jnp.where(has[i] & has_end[j], rc[2 * (1 - i) + 1 - j], jnp.zeros((8, LANES), F32))
                spread = jnp.concatenate([roll(packed, start - g * CZ) for g in range(groups)], axis=0)
                inside = lane_o < CZ if j == 0 else lane_o >= last
                extra = extra + jnp.where(inside, spread, 0.0)
        spot = pl.ds(x, cout, stride=cells_x)
        flat[spot, :] = flat[spot, :] + extra
    o_ref[...] = flat[...].reshape(cout, cells_x, LANES).astype(BF16)
    for k, (_, _, dx, dy) in enumerate(edges):

        @pl.when(exists(dx, dy))
        def _():
            edge_copy(k).wait_send()

    for copy in sent:
        copy.wait_send()


def solution(mesh):
    sizes = tuple(mesh.shape[a] for a in ("sx", "sy", "ch"))
    n_ch = sizes[2]

    def per_device(volume, weight, bias):
        cin, cells_x, merged = volume.shape
        cout = weight.shape[3]
        call = pl.pallas_call(
            lambda *refs: kernel(sizes, *refs),
            out_shape=pltpu.VMEM((cout, cells_x, merged), BF16),
            in_specs=[
                pl.BlockSpec(memory_space=pltpu.HBM),
                pl.BlockSpec(memory_space=pltpu.HBM),
                pl.BlockSpec(memory_space=pltpu.HBM),
            ],
            out_specs=pl.BlockSpec(memory_space=pltpu.VMEM),
            scratch_shapes=[
                pltpu.VMEM((3, cells_x + 2, n_ch * cin, LANES), BF16),
                pltpu.VMEM(weight.shape, BF16),
                pltpu.VMEM((cin, cells_x, LANES), BF16),
                pltpu.VMEM((1, cout), F32),
                pltpu.VMEM((cells_x + 2, 3 * cout, LANES), F32),
                pltpu.VMEM((cout * cells_x, LANES), F32),
                pltpu.VMEM((2, cout, LANES), F32),
                pltpu.VMEM((2, cout, LANES), F32),
                pltpu.VMEM((4, 8, LANES), F32),
                pltpu.VMEM((2, cout, LANES), F32),
                pltpu.VMEM((2, cout, LANES), F32),
                pltpu.VMEM((4, 8, LANES), F32),
                pltpu.SemaphoreType.DMA((2 + PARTS,)),
                pltpu.SemaphoreType.DMA((n_ch * PARTS,)),
                pltpu.SemaphoreType.DMA((n_ch * PARTS,)),
                pltpu.SemaphoreType.DMA((8,)),
                pltpu.SemaphoreType.DMA((8,)),
                pltpu.SemaphoreType.REGULAR,
            ],
            compiler_params=pltpu.CompilerParams(
                collective_id=0, has_side_effects=True, vmem_limit_bytes=32 << 20),
            name="conv_gather",
        )
        return call(*[pltpu.with_memory_space_constraint(a, pltpu.HBM) for a in (volume, weight, bias.reshape(1, cout))])

    return jax.shard_map(
        per_device,
        mesh=mesh,
        in_specs=(P("ch", "sx", "sy"), P(None, None, None, "ch", None), P("ch")),
        out_specs=P("ch", "sx", "sy"),
        check_vma=False,
    )
```

```python
import jax
import jax.numpy as jnp
from jax import lax
from jax.experimental import pallas as pl
from jax.experimental.pallas import tpu as pltpu
from jax.sharding import PartitionSpec as P

CZ = 16
LANES = 128
MESH = pl.DeviceIdType.MESH
PARTS = 2
PLAN = [
    ('turn', 0),
    ('turn', 1),
    ('send', (0, 0), 0, (1, 0)),
    ('send', (0, 0), 0, (0, 2)),
    ('send', (0, 0), 1, (1, 0)),
    ('send', (0, 0), 1, (0, 2)),
    ('send', (0, 0), 1, (0, 1)),
    ('send', (0, 0), 0, (0, 3)),
    ('send', (0, 0), 0, (0, 1)),
    ('send', (0, 0), 1, (0, 3)),
    ('own',),
    ('wait', (0, 2), 0),
    ('send', (0, 2), 0, (1, 0)),
    ('wait', (1, 0), 0),
    ('send', (1, 0), 0, (0, 1)),
    ('send', (1, 0), 0, (0, 3)),
    ('wait', (0, 2), 1),
    ('send', (0, 2), 1, (1, 0)),
    ('wait', (1, 0), 1),
    ('send', (1, 0), 1, (0, 1)),
    ('send', (1, 0), 1, (0, 3)),
    ('wait', (0, 1), 0),
    ('wait', (0, 1), 1),
    ('first', (0, 0)),
    ('wait', (0, 3), 0),
    ('wait', (0, 3), 1),
    ('next', (0, 2)),
    ('ends',),
    ('wait', (1, 1), 0),
    ('wait', (1, 1), 1),
    ('wait', (1, 3), 0),
    ('wait', (1, 3), 1),
    ('wait', (1, 2), 0),
    ('wait', (1, 2), 1),
    ('last',),
]
F32 = jnp.float32
BF16 = jnp.bfloat16


def kernel(sizes, v_hbm, w_hbm, b_hbm, o_ref, X, W, V, B, acc, ends, flat, hx, hy, hc, rx, ry, rc,
           load_sem, gs, gr, hs, hr, entered):
    n_sx, n_sy, n_ch = sizes
    half_ch = n_ch // 2
    cin, cells_x = V.shape[0], V.shape[1]
    cout = W.shape[3]
    group = half_ch * cin
    sx, sy, ch = lax.axis_index("sx"), lax.axis_index("sy"), lax.axis_index("ch")
    h, y = ch // half_ch, lax.rem(ch, half_ch)

    def member(other, k):
        across = (y, y + 1 - 2 * lax.rem(y, 2), lax.rem(y + 2, 4), 3 - y)[k]
        return (1 - h if other else h) * half_ch + across

    def mate(other, k):
        return (sx, sy, member(other, k))

    def spatial(dx, dy):
        return (sx + dx, sy + dy, ch)

    has_x = {-1: sx > 0, 0: sx >= 0, 1: sx < n_sx - 1}
    has_y = {-1: sy > 0, 0: sy >= 0, 1: sy < n_sy - 1}

    def exists(dx, dy):
        return has_x[dx] & has_y[dy]

    step_ch = cin // PARTS
    load_v = [pltpu.make_async_copy(v_hbm.at[pl.ds(p * step_ch, step_ch)], V.at[pl.ds(p * step_ch, step_ch)],
                                    load_sem.at[2 + p]) for p in range(PARTS)]
    load_w = pltpu.make_async_copy(w_hbm, W, load_sem.at[0])
    load_b = pltpu.make_async_copy(b_hbm, B, load_sem.at[1])
    for load in load_v:
        load.start()
    load_b.start()
    load_w.start()

    barrier = pltpu.get_barrier_semaphore()
    mates = sorted({step[3] for step in PLAN if step[0] == "send"})
    later = [(0, 1), (-1, 1), (1, 1), (1, 0)]
    earlier = [(-dx, -dy) for dx, dy in later]
    for m in mates:
        pl.semaphore_signal(barrier, inc=1, device_id=mate(*m), device_id_type=MESH)

    def tell(sem, places):
        for place in places:

            @pl.when(exists(*place))
            def _():
                pl.semaphore_signal(sem, inc=1, device_id=spatial(*place), device_id_type=MESH)

    def count(places):
        return sum(jnp.where(exists(*place), 1, 0) for place in places)

    tell(barrier, later)

    lane = lax.broadcasted_iota(jnp.int32, (step_ch, LANES), 1)
    z = lax.rem(lane, CZ)

    def rows(who, part):
        return pl.ds(pl.multiple_of(who * cin + part * step_ch, step_ch), step_ch)

    def turn(part):
        load_v[part].wait()
        n = step_ch * cells_x
        flat[part * n : (part + 1) * n] = V[pl.ds(part * step_ch, step_ch)].astype(F32).reshape(n, LANES)
        for x in range(cells_x):
            piece = flat[pl.ds(part * n + x, step_ch, stride=cells_x), :]
            X[1, x + 1, rows(ch, part), :] = piece.astype(BF16)

    def shift_z(who, part):
        r = rows(who, part)
        for x in range(1, cells_x + 1):
            v = X[1, x, r, :]
            X[0, x, r, :] = jnp.where(z == 0, jnp.zeros_like(v), pltpu.roll(v, 1, 1))
            X[2, x, r, :] = jnp.where(z == CZ - 1, jnp.zeros_like(v), pltpu.roll(v, LANES - 1, 1))

    last = LANES - CZ
    along_x = lane // CZ
    valid_x = (along_x >= 1, None, along_x < cells_x - 1)
    valid_z = (z >= 1, None, z < CZ - 1)

    def roll(v, by):
        by = by % LANES
        return pltpu.roll(v, by, 1) if by else v

    def pack_ends(block, part):
        r = rows(member(*block), part)
        within = lax.rem(member(*block), half_ch) * cin + part * step_ch
        to = pl.ds(pl.multiple_of(within, step_ch), step_ch)
        for e, start in enumerate((0, last)):
            packed = jnp.zeros((step_ch, LANES), BF16)
            for x in range(cells_x):
                packed = jnp.where(along_x == x, roll(X[1, x + 1, r, :], x * CZ - start), packed)
            for a in range(3):
                for c in range(3):
                    v = roll(packed, (1 - a) * CZ + 1 - c)
                    for valid in (valid_x[a], valid_z[c]):
                        if valid is not None:
                            v = jnp.where(valid, v, jnp.zeros_like(v))
                    ends[e, 3 * a + c, to, :] = v

    def block_copy(block, part, out, slot, to):
        piece = X.at[1, 1 : cells_x + 1, rows(member(*block), part), :]
        return pltpu.make_async_remote_copy(
            src_ref=piece, dst_ref=piece, send_sem=gs.at[out], recv_sem=gr.at[slot],
            device_id=mate(*to), device_id_type=MESH)

    sent = []

    def send(block, part, to):
        other, k = block[0] ^ to[0], block[1] ^ to[1]
        copy = block_copy(block, part, len(sent), (other * half_ch + k) * PARTS + part, to)
        copy.start()
        sent.append(copy)

    def arrived(block, part):
        block_copy(block, part, 0, (block[0] * half_ch + block[1]) * PARTS + part, (1, 0)).wait_recv()

    pair = 2 * cin

    def pair_of(block):
        return pl.ds(pl.multiple_of(member(*block) // 2 * pair, pair), pair)

    ends_x = [(0,), (cells_x + 1,)]
    inside = [(x, x + 1) for x in range(1, cells_x + 1, 2)]

    def products(cols, first, spans):
        for slabs in spans:
            taps = [a for a in range(3) if any(0 < o + a - 1 < cells_x + 1 for o in slabs)]
            lhs = jnp.concatenate(
                [W[a, :, c, :, cols].reshape(3 * cout, cols.size) for a in taps for c in range(3)], axis=1)
            rhs = jnp.concatenate(
                [jnp.concatenate([X[c, o + a - 1, cols, :] for o in slabs], axis=1)
                 for a in taps for c in range(3)], axis=0)
            r = jnp.dot(lhs, rhs, preferred_element_type=F32)
            for j, o in enumerate(slabs):
                part = r[:, LANES * j : LANES * (j + 1)]
                acc[o] = part if first else acc[o] + part

    lane_o = lax.broadcasted_iota(jnp.int32, (cout, LANES), 1)

    def taps_of(s, b):
        return acc[s, b * cout : (b + 1) * cout]

    def along_y(s):
        up = jnp.where(lane_o < CZ, 0.0, pltpu.roll(taps_of(s, 0), CZ, 1))
        down = jnp.where(lane_o >= last, 0.0, pltpu.roll(taps_of(s, 2), LANES - CZ, 1))
        return taps_of(s, 1) + up + down

    groups = cout // 8
    lane_8 = lax.broadcasted_iota(jnp.int32, (8, LANES), 1)
    def corners():
        for i, s in enumerate((0, cells_x + 1)):
            for j, (b, start) in enumerate(((2, 0), (0, last))):
                corner = jnp.zeros((8, LANES), F32)
                for g in range(groups):
                    here = (lane_8 >= g * CZ) & (lane_8 < (g + 1) * CZ)
                    piece = acc[s, b * cout + 8 * g : b * cout + 8 * g + 8]
                    corner = jnp.where(here, roll(piece, g * CZ - start), corner)
                hc[2 * i + j] = corner

    def ends_so_far():
        low = jnp.zeros((cout, LANES), F32)
        high = jnp.zeros((cout, LANES), F32)
        for x in range(cells_x):
            here = (lane_o >= x * CZ) & (lane_o < (x + 1) * CZ)
            low = jnp.where(here, roll(taps_of(x + 1, 2), x * CZ), low)
            high = jnp.where(here, roll(taps_of(x + 1, 0), x * CZ - last), high)
        hy[0] = low
        hy[1] = high

    far_half = pl.ds(pl.multiple_of((1 - h) * group, group), group)

    def ends_of(cols):
        for e, b in enumerate((2, 0)):
            lhs = jnp.concatenate([W[a, b, c, :, cols] for a in range(3) for c in range(3)], axis=1)
            rhs = jnp.concatenate([ends[e, t] for t in range(9)], axis=0)
            hy[e] = hy[e] + jnp.dot(lhs, rhs, preferred_element_type=F32)

    edges = [(hy.at[0], ry.at[0], 0, -1), (hy.at[1], ry.at[1], 0, 1),
             (hx.at[0], rx.at[0], -1, 0), (hx.at[1], rx.at[1], 1, 0)]
    edges += [(hc.at[2 * i + j], rc.at[2 * i + j], dx, dy)
              for i, dx in enumerate((-1, 1)) for j, dy in enumerate((-1, 1))]

    def edge_copy(k):
        src, dst, dx, dy = edges[k]
        return pltpu.make_async_remote_copy(
            src_ref=src, dst_ref=dst, send_sem=hs.at[k], recv_sem=hr.at[k],
            device_id=spatial(dx, dy), device_id_type=MESH)

    def leave(ks):
        for k in ks:

            @pl.when(exists(*edges[k][2:]))
            def _():
                edge_copy(k).start()

    ready = False
    for step in PLAN:
        if step[0] == "turn":
            turn(step[1])
        elif step[0] == "send":
            if not ready:
                pl.semaphore_wait(barrier, len(mates) + count(earlier))
                ready = True
            send(*step[1:])
        elif step[0] == "wait":
            arrived(*step[1:])
            if step[1][0] == 1:
                pack_ends(*step[1:])
            if step[1] != (1, 2):
                shift_z(member(*step[1]), step[2])
        elif step[0] == "ends":
            ends_so_far()
        elif step[0] == "own":
            tell(entered, earlier)
            zero = jnp.zeros((n_ch * cin, LANES), BF16)
            for c in range(3):
                X[c, 0] = zero
                X[c, cells_x + 1] = zero
            for part in range(PARTS):
                shift_z(ch, part)
        elif step[0] == "first":
            load_w.wait()
            load_b.wait()
            products(pair_of(step[1]), True, ends_x + inside)
        elif step[0] == "next":
            products(pair_of(step[1]), False, ends_x + inside)
        else:
            ends_of(far_half)
            some = count(later)

            @pl.when(some > 0)
            def _():
                pl.semaphore_wait(entered, some)

            leave(range(2))
            for part in range(PARTS):
                shift_z(member(1, 2), part)
            products(far_half, False, ends_x)
            corners()
            leave(range(4, 8))
            hx[0] = along_y(0)
            hx[1] = along_y(cells_x + 1)
            leave(range(2, 4))


    products(far_half, False, inside)
    sub = lax.broadcasted_iota(jnp.int32, (cout, cout), 0)
    across = lax.broadcasted_iota(jnp.int32, (cout, cout), 1)
    bias = jnp.sum(jnp.where(sub == across, jnp.broadcast_to(B[...], (cout, cout)), 0.0),
                   axis=1, keepdims=True)
    for x in range(cells_x):
        flat[pl.ds(x, cout, stride=cells_x), :] = along_y(x + 1) + bias

    for k, (_, _, dx, dy) in enumerate(edges):

        @pl.when(exists(-dx, -dy))
        def _():
            edge_copy(k).wait_recv()

    has, has_end = (has_x[-1], has_x[1]), (has_y[-1], has_y[1])
    zeros = jnp.zeros((cout, LANES), F32)
    from_low_y = jnp.where(has_end[0], ry[1], zeros)
    from_high_y = jnp.where(has_end[1], ry[0], zeros)
    for x in range(cells_x):
        extra = jnp.where(lane_o < CZ, roll(from_low_y, -x * CZ), 0.0)
        extra = jnp.where(lane_o >= last, roll(from_high_y, last - x * CZ), extra)
        if x in (0, cells_x - 1):
            i = 0 if x == 0 else 1
            extra = extra + jnp.where(has[i], rx[1 - i], zeros)
            corners = []
            for j in range(2):
                start = 0 if j == 0 else last
                packed = jnp.where(has[i] & has_end[j], rc[2 * (1 - i) + 1 - j], jnp.zeros((8, LANES), F32))
                spread = jnp.concatenate([roll(packed, start - g * CZ) for g in range(groups)], axis=0)
                inside = lane_o < CZ if j == 0 else lane_o >= last
                extra = extra + jnp.where(inside, spread, 0.0)
        spot = pl.ds(x, cout, stride=cells_x)
        flat[spot, :] = flat[spot, :] + extra
    o_ref[...] = flat[...].reshape(cout, cells_x, LANES).astype(BF16)
    for k, (_, _, dx, dy) in enumerate(edges):

        @pl.when(exists(dx, dy))
        def _():
            edge_copy(k).wait_send()

    for copy in sent:
        copy.wait_send()


def solution(mesh):
    sizes = tuple(mesh.shape[a] for a in ("sx", "sy", "ch"))
    n_ch = sizes[2]

    def per_device(volume, weight, bias):
        cin, cells_x, merged = volume.shape
        cout = weight.shape[3]
        call = pl.pallas_call(
            lambda *refs: kernel(sizes, *refs),
            out_shape=pltpu.VMEM((cout, cells_x, merged), BF16),
            in_specs=[
                pl.BlockSpec(memory_space=pltpu.HBM),
                pl.BlockSpec(memory_space=pltpu.HBM),
                pl.BlockSpec(memory_space=pltpu.HBM),
            ],
            out_specs=pl.BlockSpec(memory_space=pltpu.VMEM),
            scratch_shapes=[
                pltpu.VMEM((3, cells_x + 2, n_ch * cin, LANES), BF16),
                pltpu.VMEM(weight.shape, BF16),
                pltpu.VMEM((cin, cells_x, LANES), BF16),
                pltpu.VMEM((1, cout), F32),
                pltpu.VMEM((cells_x + 2, 3 * cout, LANES), F32),
                pltpu.VMEM((2, 9, n_ch // 2 * cin, LANES), BF16),
                pltpu.VMEM((cout * cells_x, LANES), F32),
                pltpu.VMEM((2, cout, LANES), F32),
                pltpu.VMEM((2, cout, LANES), F32),
                pltpu.VMEM((4, 8, LANES), F32),
                pltpu.VMEM((2, cout, LANES), F32),
                pltpu.VMEM((2, cout, LANES), F32),
                pltpu.VMEM((4, 8, LANES), F32),
                pltpu.SemaphoreType.DMA((2 + PARTS,)),
                pltpu.SemaphoreType.DMA((n_ch * PARTS,)),
                pltpu.SemaphoreType.DMA((n_ch * PARTS,)),
                pltpu.SemaphoreType.DMA((8,)),
                pltpu.SemaphoreType.DMA((8,)),
                pltpu.SemaphoreType.REGULAR,
            ],
            compiler_params=pltpu.CompilerParams(
                collective_id=0, has_side_effects=True, vmem_limit_bytes=32 << 20),
            name="conv_gather",
        )
        return call(*[pltpu.with_memory_space_constraint(a, pltpu.HBM) for a in (volume, weight, bias.reshape(1, cout))])

    return jax.shard_map(
        per_device,
        mesh=mesh,
        in_specs=(P("ch", "sx", "sy"), P(None, None, None, "ch", None), P("ch")),
        out_specs=P("ch", "sx", "sy"),
        check_vma=False,
    )
```

```python
import jax
import jax.numpy as jnp
from jax import lax
from jax.experimental import pallas as pl
from jax.experimental.pallas import tpu as pltpu
from jax.sharding import PartitionSpec as P

CZ = 16
LANES = 128
MESH = pl.DeviceIdType.MESH
PARTS = 2
PLAN = [
    ('turn', 0),
    ('send', (0, 0), 0, (1, 0)),
    ('send', (0, 0), 0, (0, 2)),
    ('turn', 1),
    ('send', (0, 0), 1, (1, 0)),
    ('send', (0, 0), 1, (0, 2)),
    ('send', (0, 0), 1, (0, 1)),
    ('send', (0, 0), 0, (0, 3)),
    ('send', (0, 0), 0, (0, 1)),
    ('send', (0, 0), 1, (0, 3)),
    ('own',),
    ('wait', (0, 2), 0),
    ('send', (0, 2), 0, (1, 0)),
    ('wait', (1, 0), 0),
    ('send', (1, 0), 0, (0, 1)),
    ('send', (1, 0), 0, (0, 3)),
    ('wait', (0, 2), 1),
    ('send', (0, 2), 1, (1, 0)),
    ('wait', (1, 0), 1),
    ('send', (1, 0), 1, (0, 1)),
    ('send', (1, 0), 1, (0, 3)),
    ('wait', (0, 1), 0),
    ('wait', (0, 1), 1),
    ('first', (0, 0)),
    ('wait', (0, 3), 0),
    ('wait', (0, 3), 1),
    ('next', (0, 2)),
    ('ends',),
    ('wait', (1, 1), 0),
    ('wait', (1, 1), 1),
    ('wait', (1, 3), 0),
    ('wait', (1, 3), 1),
    ('wait', (1, 2), 0),
    ('wait', (1, 2), 1),
    ('last',),
]
F32 = jnp.float32
BF16 = jnp.bfloat16


def kernel(sizes, v_hbm, w_hbm, b_hbm, o_ref, X, W, V, B, acc, ends, flat, hx, hy, hc, rx, ry, rc,
           load_sem, gs, gr, hs, hr, entered):
    n_sx, n_sy, n_ch = sizes
    half_ch = n_ch // 2
    cin, cells_x = V.shape[0], V.shape[1]
    cout = W.shape[3]
    group = half_ch * cin
    sx, sy, ch = lax.axis_index("sx"), lax.axis_index("sy"), lax.axis_index("ch")
    h, y = ch // half_ch, lax.rem(ch, half_ch)

    def member(other, k):
        across = (y, y + 1 - 2 * lax.rem(y, 2), lax.rem(y + 2, 4), 3 - y)[k]
        return (1 - h if other else h) * half_ch + across

    def mate(other, k):
        return (sx, sy, member(other, k))

    def spatial(dx, dy):
        return (sx + dx, sy + dy, ch)

    has_x = {-1: sx > 0, 0: sx >= 0, 1: sx < n_sx - 1}
    has_y = {-1: sy > 0, 0: sy >= 0, 1: sy < n_sy - 1}

    def exists(dx, dy):
        return has_x[dx] & has_y[dy]

    step_ch = cin // PARTS
    load_v = [pltpu.make_async_copy(v_hbm.at[pl.ds(p * step_ch, step_ch)], V.at[pl.ds(p * step_ch, step_ch)],
                                    load_sem.at[2 + p]) for p in range(PARTS)]
    load_w = pltpu.make_async_copy(w_hbm, W, load_sem.at[0])
    load_b = pltpu.make_async_copy(b_hbm, B, load_sem.at[1])
    for load in load_v:
        load.start()
    load_b.start()
    load_w.start()

    barrier = pltpu.get_barrier_semaphore()
    mates = sorted({step[3] for step in PLAN if step[0] == "send"})
    later = [(0, 1), (-1, 1), (1, 1), (1, 0)]
    earlier = [(-dx, -dy) for dx, dy in later]
    for m in mates:
        pl.semaphore_signal(barrier, inc=1, device_id=mate(*m), device_id_type=MESH)

    def tell(sem, places):
        for place in places:

            @pl.when(exists(*place))
            def _():
                pl.semaphore_signal(sem, inc=1, device_id=spatial(*place), device_id_type=MESH)

    def count(places):
        return sum(jnp.where(exists(*place), 1, 0) for place in places)

    tell(barrier, later)

    lane = lax.broadcasted_iota(jnp.int32, (step_ch, LANES), 1)
    z = lax.rem(lane, CZ)

    def rows(who, part):
        return pl.ds(pl.multiple_of(who * cin + part * step_ch, step_ch), step_ch)

    def turn(part):
        load_v[part].wait()
        n = step_ch * cells_x
        flat[part * n : (part + 1) * n] = V[pl.ds(part * step_ch, step_ch)].astype(F32).reshape(n, LANES)
        for x in range(cells_x):
            piece = flat[pl.ds(part * n + x, step_ch, stride=cells_x), :]
            X[1, x + 1, rows(ch, part), :] = piece.astype(BF16)

    def shift_z(who, part):
        r = rows(who, part)
        for x in range(1, cells_x + 1):
            v = X[1, x, r, :]
            X[0, x, r, :] = jnp.where(z == 0, jnp.zeros_like(v), pltpu.roll(v, 1, 1))
            X[2, x, r, :] = jnp.where(z == CZ - 1, jnp.zeros_like(v), pltpu.roll(v, LANES - 1, 1))

    last = LANES - CZ
    along_x = lane // CZ
    valid_x = (along_x >= 1, None, along_x < cells_x - 1)
    valid_z = (z >= 1, None, z < CZ - 1)

    def roll(v, by):
        by = by % LANES
        return pltpu.roll(v, by, 1) if by else v

    def pack_ends(block, part):
        r = rows(member(*block), part)
        within = lax.rem(member(*block), half_ch) * cin + part * step_ch
        to = pl.ds(pl.multiple_of(within, step_ch), step_ch)
        for e, start in enumerate((0, last)):
            packed = jnp.zeros((step_ch, LANES), BF16)
            for x in range(cells_x):
                packed = jnp.where(along_x == x, roll(X[1, x + 1, r, :], x * CZ - start), packed)
            for a in range(3):
                for c in range(3):
                    v = roll(packed, (1 - a) * CZ + 1 - c)
                    for valid in (valid_x[a], valid_z[c]):
                        if valid is not None:
                            v = jnp.where(valid, v, jnp.zeros_like(v))
                    ends[e, 3 * a + c, to, :] = v

    def block_copy(block, part, out, slot, to):
        piece = X.at[1, 1 : cells_x + 1, rows(member(*block), part), :]
        return pltpu.make_async_remote_copy(
            src_ref=piece, dst_ref=piece, send_sem=gs.at[out], recv_sem=gr.at[slot],
            device_id=mate(*to), device_id_type=MESH)

    sent = []

    def send(block, part, to):
        other, k = block[0] ^ to[0], block[1] ^ to[1]
        copy = block_copy(block, part, len(sent), (other * half_ch + k) * PARTS + part, to)
        copy.start()
        sent.append(copy)

    def arrived(block, part):
        block_copy(block, part, 0, (block[0] * half_ch + block[1]) * PARTS + part, (1, 0)).wait_recv()

    pair = 2 * cin

    def pair_of(block):
        return pl.ds(pl.multiple_of(member(*block) // 2 * pair, pair), pair)

    ends_x = [(0,), (cells_x + 1,)]
    inside = [(x, x + 1) for x in range(1, cells_x + 1, 2)]

    def products(cols, first, spans):
        for slabs in spans:
            taps = [a for a in range(3) if any(0 < o + a - 1 < cells_x + 1 for o in slabs)]
            lhs = jnp.concatenate(
                [W[a, :, c, :, cols].reshape(3 * cout, cols.size) for a in taps for c in range(3)], axis=1)
            rhs = jnp.concatenate(
                [jnp.concatenate([X[c, o + a - 1, cols, :] for o in slabs], axis=1)
                 for a in taps for c in range(3)], axis=0)
            r = jnp.dot(lhs, rhs, preferred_element_type=F32)
            for j, o in enumerate(slabs):
                part = r[:, LANES * j : LANES * (j + 1)]
                acc[o] = part if first else acc[o] + part

    lane_o = lax.broadcasted_iota(jnp.int32, (cout, LANES), 1)

    def taps_of(s, b):
        return acc[s, b * cout : (b + 1) * cout]

    def along_y(s):
        up = jnp.where(lane_o < CZ, 0.0, pltpu.roll(taps_of(s, 0), CZ, 1))
        down = jnp.where(lane_o >= last, 0.0, pltpu.roll(taps_of(s, 2), LANES - CZ, 1))
        return taps_of(s, 1) + up + down

    groups = cout // 8
    lane_8 = lax.broadcasted_iota(jnp.int32, (8, LANES), 1)
    def corners():
        for i, s in enumerate((0, cells_x + 1)):
            for j, (b, start) in enumerate(((2, 0), (0, last))):
                corner = jnp.zeros((8, LANES), F32)
                for g in range(groups):
                    here = (lane_8 >= g * CZ) & (lane_8 < (g + 1) * CZ)
                    piece = acc[s, b * cout + 8 * g : b * cout + 8 * g + 8]
                    corner = jnp.where(here, roll(piece, g * CZ - start), corner)
                hc[2 * i + j] = corner

    def ends_so_far():
        low = jnp.zeros((cout, LANES), F32)
        high = jnp.zeros((cout, LANES), F32)
        for x in range(cells_x):
            here = (lane_o >= x * CZ) & (lane_o < (x + 1) * CZ)
            low = jnp.where(here, roll(taps_of(x + 1, 2), x * CZ), low)
            high = jnp.where(here, roll(taps_of(x + 1, 0), x * CZ - last), high)
        hy[0] = low
        hy[1] = high

    far_half = pl.ds(pl.multiple_of((1 - h) * group, group), group)

    def ends_of(cols):
        for e, b in enumerate((2, 0)):
            lhs = jnp.concatenate([W[a, b, c, :, cols] for a in range(3) for c in range(3)], axis=1)
            rhs = jnp.concatenate([ends[e, t] for t in range(9)], axis=0)
            hy[e] = hy[e] + jnp.dot(lhs, rhs, preferred_element_type=F32)

    edges = [(hy.at[0], ry.at[0], 0, -1), (hy.at[1], ry.at[1], 0, 1),
             (hx.at[0], rx.at[0], -1, 0), (hx.at[1], rx.at[1], 1, 0)]
    edges += [(hc.at[2 * i + j], rc.at[2 * i + j], dx, dy)
              for i, dx in enumerate((-1, 1)) for j, dy in enumerate((-1, 1))]

    def edge_copy(k):
        src, dst, dx, dy = edges[k]
        return pltpu.make_async_remote_copy(
            src_ref=src, dst_ref=dst, send_sem=hs.at[k], recv_sem=hr.at[k],
            device_id=spatial(dx, dy), device_id_type=MESH)

    def leave(ks):
        for k in ks:

            @pl.when(exists(*edges[k][2:]))
            def _():
                edge_copy(k).start()

    ready = False
    for step in PLAN:
        if step[0] == "turn":
            turn(step[1])
        elif step[0] == "send":
            if not ready:
                pl.semaphore_wait(barrier, len(mates) + count(earlier))
                ready = True
            send(*step[1:])
        elif step[0] == "wait":
            arrived(*step[1:])
            if step[1][0] == 1:
                pack_ends(*step[1:])
            if step[1] != (1, 2):
                shift_z(member(*step[1]), step[2])
        elif step[0] == "ends":
            ends_so_far()
        elif step[0] == "own":
            tell(entered, earlier)
            zero = jnp.zeros((n_ch * cin, LANES), BF16)
            for c in range(3):
                X[c, 0] = zero
                X[c, cells_x + 1] = zero
            for part in range(PARTS):
                shift_z(ch, part)
        elif step[0] == "first":
            load_w.wait()
            load_b.wait()
            products(pair_of(step[1]), True, ends_x + inside)
        elif step[0] == "next":
            products(pair_of(step[1]), False, ends_x + inside)
        else:
            ends_of(far_half)
            some = count(later)

            @pl.when(some > 0)
            def _():
                pl.semaphore_wait(entered, some)

            leave(range(2))
            for part in range(PARTS):
                shift_z(member(1, 2), part)
            products(far_half, False, ends_x)
            corners()
            leave(range(4, 8))
            hx[0] = along_y(0)
            hx[1] = along_y(cells_x + 1)
            leave(range(2, 4))


    products(far_half, False, inside)
    sub = lax.broadcasted_iota(jnp.int32, (cout, cout), 0)
    across = lax.broadcasted_iota(jnp.int32, (cout, cout), 1)
    bias = jnp.sum(jnp.where(sub == across, jnp.broadcast_to(B[...], (cout, cout)), 0.0),
                   axis=1, keepdims=True)
    for x in range(cells_x):
        flat[pl.ds(x, cout, stride=cells_x), :] = along_y(x + 1) + bias

    for k, (_, _, dx, dy) in enumerate(edges):

        @pl.when(exists(-dx, -dy))
        def _():
            edge_copy(k).wait_recv()

    has, has_end = (has_x[-1], has_x[1]), (has_y[-1], has_y[1])
    zeros = jnp.zeros((cout, LANES), F32)
    from_low_y = jnp.where(has_end[0], ry[1], zeros)
    from_high_y = jnp.where(has_end[1], ry[0], zeros)
    for x in range(cells_x):
        extra = jnp.where(lane_o < CZ, roll(from_low_y, -x * CZ), 0.0)
        extra = jnp.where(lane_o >= last, roll(from_high_y, last - x * CZ), extra)
        if x in (0, cells_x - 1):
            i = 0 if x == 0 else 1
            extra = extra + jnp.where(has[i], rx[1 - i], zeros)
            corners = []
            for j in range(2):
                start = 0 if j == 0 else last
                packed = jnp.where(has[i] & has_end[j], rc[2 * (1 - i) + 1 - j], jnp.zeros((8, LANES), F32))
                spread = jnp.concatenate([roll(packed, start - g * CZ) for g in range(groups)], axis=0)
                inside = lane_o < CZ if j == 0 else lane_o >= last
                extra = extra + jnp.where(inside, spread, 0.0)
        spot = pl.ds(x, cout, stride=cells_x)
        flat[spot, :] = flat[spot, :] + extra
    o_ref[...] = flat[...].reshape(cout, cells_x, LANES).astype(BF16)
    for k, (_, _, dx, dy) in enumerate(edges):

        @pl.when(exists(dx, dy))
        def _():
            edge_copy(k).wait_send()

    for copy in sent:
        copy.wait_send()


def solution(mesh):
    sizes = tuple(mesh.shape[a] for a in ("sx", "sy", "ch"))
    n_ch = sizes[2]

    def per_device(volume, weight, bias):
        cin, cells_x, merged = volume.shape
        cout = weight.shape[3]
        call = pl.pallas_call(
            lambda *refs: kernel(sizes, *refs),
            out_shape=pltpu.VMEM((cout, cells_x, merged), BF16),
            in_specs=[
                pl.BlockSpec(memory_space=pltpu.HBM),
                pl.BlockSpec(memory_space=pltpu.HBM),
                pl.BlockSpec(memory_space=pltpu.HBM),
            ],
            out_specs=pl.BlockSpec(memory_space=pltpu.VMEM),
            scratch_shapes=[
                pltpu.VMEM((3, cells_x + 2, n_ch * cin, LANES), BF16),
                pltpu.VMEM(weight.shape, BF16),
                pltpu.VMEM((cin, cells_x, LANES), BF16),
                pltpu.VMEM((1, cout), F32),
                pltpu.VMEM((cells_x + 2, 3 * cout, LANES), F32),
                pltpu.VMEM((2, 9, n_ch // 2 * cin, LANES), BF16),
                pltpu.VMEM((cout * cells_x, LANES), F32),
                pltpu.VMEM((2, cout, LANES), F32),
                pltpu.VMEM((2, cout, LANES), F32),
                pltpu.VMEM((4, 8, LANES), F32),
                pltpu.VMEM((2, cout, LANES), F32),
                pltpu.VMEM((2, cout, LANES), F32),
                pltpu.VMEM((4, 8, LANES), F32),
                pltpu.SemaphoreType.DMA((2 + PARTS,)),
                pltpu.SemaphoreType.DMA((n_ch * PARTS,)),
                pltpu.SemaphoreType.DMA((n_ch * PARTS,)),
                pltpu.SemaphoreType.DMA((8,)),
                pltpu.SemaphoreType.DMA((8,)),
                pltpu.SemaphoreType.REGULAR,
            ],
            compiler_params=pltpu.CompilerParams(
                collective_id=0, has_side_effects=True, vmem_limit_bytes=32 << 20),
            name="conv_gather",
        )
        return call(*[pltpu.with_memory_space_constraint(a, pltpu.HBM) for a in (volume, weight, bias.reshape(1, cout))])

    return jax.shard_map(
        per_device,
        mesh=mesh,
        in_specs=(P("ch", "sx", "sy"), P(None, None, None, "ch", None), P("ch")),
        out_specs=P("ch", "sx", "sy"),
        check_vma=False,
    )
```

```python
import jax
import jax.numpy as jnp
from jax import lax
from jax.experimental import pallas as pl
from jax.experimental.pallas import tpu as pltpu
from jax.sharding import PartitionSpec as P

CZ = 16
LANES = 128
MESH = pl.DeviceIdType.MESH
PARTS = 2
PLAN = [
    ('turn', 0),
    ('turn', 1),
    ('send', (0, 0), 0, (1, 0)),
    ('send', (0, 0), 0, (0, 2)),
    ('send', (0, 0), 1, (1, 0)),
    ('send', (0, 0), 1, (0, 2)),
    ('send', (0, 0), 1, (0, 1)),
    ('send', (0, 0), 0, (0, 3)),
    ('send', (0, 0), 0, (0, 1)),
    ('send', (0, 0), 1, (0, 3)),
    ('own',),
    ('wait', (0, 2), 0),
    ('send', (0, 2), 0, (1, 0)),
    ('wait', (1, 0), 0),
    ('send', (1, 0), 0, (0, 1)),
    ('send', (1, 0), 0, (0, 3)),
    ('wait', (0, 2), 1),
    ('send', (0, 2), 1, (1, 0)),
    ('wait', (1, 0), 1),
    ('send', (1, 0), 1, (0, 1)),
    ('send', (1, 0), 1, (0, 3)),
    ('wait', (0, 1), 0),
    ('wait', (0, 1), 1),
    ('first', (0, 0)),
    ('wait', (0, 3), 0),
    ('wait', (0, 3), 1),
    ('next', (0, 2)),
    ('ends',),
    ('wait', (1, 1), 0),
    ('wait', (1, 1), 1),
    ('wait', (1, 3), 0),
    ('wait', (1, 3), 1),
    ('wait', (1, 2), 0),
    ('wait', (1, 2), 1),
    ('last',),
]
F32 = jnp.float32
BF16 = jnp.bfloat16


def kernel(sizes, v_hbm, w_hbm, b_hbm, o_ref, X, W, V, B, acc, ends, flat, hx, hy, hc, rx, ry, rc,
           load_sem, gs, gr, hs, hr, entered):
    n_sx, n_sy, n_ch = sizes
    half_ch = n_ch // 2
    cin, cells_x = V.shape[0], V.shape[1]
    cout = W.shape[3]
    group = half_ch * cin
    sx, sy, ch = lax.axis_index("sx"), lax.axis_index("sy"), lax.axis_index("ch")
    h, y = ch // half_ch, lax.rem(ch, half_ch)

    def member(other, k):
        across = (y, y + 1 - 2 * lax.rem(y, 2), lax.rem(y + 2, 4), 3 - y)[k]
        return (1 - h if other else h) * half_ch + across

    def mate(other, k):
        return (sx, sy, member(other, k))

    def spatial(dx, dy):
        return (sx + dx, sy + dy, ch)

    has_x = {-1: sx > 0, 0: sx >= 0, 1: sx < n_sx - 1}
    has_y = {-1: sy > 0, 0: sy >= 0, 1: sy < n_sy - 1}

    def exists(dx, dy):
        return has_x[dx] & has_y[dy]

    step_ch = cin // PARTS
    load_v = [pltpu.make_async_copy(v_hbm.at[pl.ds(p * step_ch, step_ch)], V.at[pl.ds(p * step_ch, step_ch)],
                                    load_sem.at[2 + p]) for p in range(PARTS)]
    load_w = pltpu.make_async_copy(w_hbm, W, load_sem.at[0])
    load_b = pltpu.make_async_copy(b_hbm, B, load_sem.at[1])
    for load in load_v:
        load.start()
    load_b.start()
    load_w.start()

    barrier = pltpu.get_barrier_semaphore()
    mates = sorted({step[3] for step in PLAN if step[0] == "send"})
    later = [(0, 1), (-1, 1), (1, 1), (1, 0)]
    earlier = [(-dx, -dy) for dx, dy in later]
    for m in mates:
        pl.semaphore_signal(barrier, inc=1, device_id=mate(*m), device_id_type=MESH)

    def tell(sem, places):
        for place in places:

            @pl.when(exists(*place))
            def _():
                pl.semaphore_signal(sem, inc=1, device_id=spatial(*place), device_id_type=MESH)

    def count(places):
        return sum(jnp.where(exists(*place), 1, 0) for place in places)

    tell(barrier, later)

    lane = lax.broadcasted_iota(jnp.int32, (step_ch, LANES), 1)
    z = lax.rem(lane, CZ)

    def rows(who, part):
        return pl.ds(pl.multiple_of(who * cin + part * step_ch, step_ch), step_ch)

    def turn(part):
        load_v[part].wait()
        n = step_ch * cells_x
        flat[part * n : (part + 1) * n] = V[pl.ds(part * step_ch, step_ch)].astype(F32).reshape(n, LANES)
        for x in range(cells_x):
            piece = flat[pl.ds(part * n + x, step_ch, stride=cells_x), :]
            X[1, x + 1, rows(ch, part), :] = piece.astype(BF16)

    def shift_z(who, part):
        r = rows(who, part)
        for x in range(1, cells_x + 1):
            v = X[1, x, r, :]
            X[0, x, r, :] = jnp.where(z == 0, jnp.zeros_like(v), pltpu.roll(v, 1, 1))
            X[2, x, r, :] = jnp.where(z == CZ - 1, jnp.zeros_like(v), pltpu.roll(v, LANES - 1, 1))

    last = LANES - CZ
    along_x = lane // CZ
    valid_x = (along_x >= 1, None, along_x < cells_x - 1)
    valid_z = (z >= 1, None, z < CZ - 1)

    def roll(v, by):
        by = by % LANES
        return pltpu.roll(v, by, 1) if by else v

    def pack_ends(block, part):
        r = rows(member(*block), part)
        within = lax.rem(member(*block), half_ch) * cin + part * step_ch
        to = pl.ds(pl.multiple_of(within, step_ch), step_ch)
        for e, start in enumerate((0, last)):
            packed = jnp.zeros((step_ch, LANES), BF16)
            for x in range(cells_x):
                packed = jnp.where(along_x == x, roll(X[1, x + 1, r, :], x * CZ - start), packed)
            for a in range(3):
                for c in range(3):
                    v = roll(packed, (1 - a) * CZ + 1 - c)
                    for valid in (valid_x[a], valid_z[c]):
                        if valid is not None:
                            v = jnp.where(valid, v, jnp.zeros_like(v))
                    ends[e, 3 * a + c, to, :] = v

    def block_copy(block, part, out, slot, to):
        piece = X.at[1, 1 : cells_x + 1, rows(member(*block), part), :]
        return pltpu.make_async_remote_copy(
            src_ref=piece, dst_ref=piece, send_sem=gs.at[out], recv_sem=gr.at[slot],
            device_id=mate(*to), device_id_type=MESH)

    sent = []

    def send(block, part, to):
        other, k = block[0] ^ to[0], block[1] ^ to[1]
        copy = block_copy(block, part, len(sent), (other * half_ch + k) * PARTS + part, to)
        copy.start()
        sent.append(copy)

    def arrived(block, part):
        block_copy(block, part, 0, (block[0] * half_ch + block[1]) * PARTS + part, (1, 0)).wait_recv()

    pair = 2 * cin

    def pair_of(block):
        return pl.ds(pl.multiple_of(member(*block) // 2 * pair, pair), pair)

    ends_x = [(0,), (cells_x + 1,)]
    inside = [(x, x + 1) for x in range(1, cells_x + 1, 2)]

    def products(cols, first, spans):
        for slabs in spans:
            taps = [a for a in range(3) if any(0 < o + a - 1 < cells_x + 1 for o in slabs)]
            lhs = jnp.concatenate(
                [W[a, :, c, :, cols].reshape(3 * cout, cols.size) for a in taps for c in range(3)], axis=1)
            rhs = jnp.concatenate(
                [jnp.concatenate([X[c, o + a - 1, cols, :] for o in slabs], axis=1)
                 for a in taps for c in range(3)], axis=0)
            r = jnp.dot(lhs, rhs, preferred_element_type=F32)
            for j, o in enumerate(slabs):
                part = r[:, LANES * j : LANES * (j + 1)]
                acc[o] = part if first else acc[o] + part

    lane_o = lax.broadcasted_iota(jnp.int32, (cout, LANES), 1)

    def taps_of(s, b):
        return acc[s, b * cout : (b + 1) * cout]

    def along_y(s):
        up = jnp.where(lane_o < CZ, 0.0, pltpu.roll(taps_of(s, 0), CZ, 1))
        down = jnp.where(lane_o >= last, 0.0, pltpu.roll(taps_of(s, 2), LANES - CZ, 1))
        return taps_of(s, 1) + up + down

    groups = cout // 8
    lane_8 = lax.broadcasted_iota(jnp.int32, (8, LANES), 1)
    def corners():
        for i, s in enumerate((0, cells_x + 1)):
            for j, (b, start) in enumerate(((2, 0), (0, last))):
                corner = jnp.zeros((8, LANES), F32)
                for g in range(groups):
                    here = (lane_8 >= g * CZ) & (lane_8 < (g + 1) * CZ)
                    piece = acc[s, b * cout + 8 * g : b * cout + 8 * g + 8]
                    corner = jnp.where(here, roll(piece, g * CZ - start), corner)
                hc[2 * i + j] = corner

    def ends_so_far():
        low = jnp.zeros((cout, LANES), F32)
        high = jnp.zeros((cout, LANES), F32)
        for x in range(cells_x):
            here = (lane_o >= x * CZ) & (lane_o < (x + 1) * CZ)
            low = jnp.where(here, roll(taps_of(x + 1, 2), x * CZ), low)
            high = jnp.where(here, roll(taps_of(x + 1, 0), x * CZ - last), high)
        hy[0] = low
        hy[1] = high

    far_half = pl.ds(pl.multiple_of((1 - h) * group, group), group)

    def ends_of(cols):
        for e, b in enumerate((2, 0)):
            lhs = jnp.concatenate([W[a, b, c, :, cols] for a in range(3) for c in range(3)], axis=1)
            rhs = jnp.concatenate([ends[e, t] for t in range(9)], axis=0)
            hy[e] = hy[e] + jnp.dot(lhs, rhs, preferred_element_type=F32)

    edges = [(hy.at[0], ry.at[0], 0, -1), (hy.at[1], ry.at[1], 0, 1),
             (hx.at[0], rx.at[0], -1, 0), (hx.at[1], rx.at[1], 1, 0)]
    edges += [(hc.at[2 * i + j], rc.at[2 * i + j], dx, dy)
              for i, dx in enumerate((-1, 1)) for j, dy in enumerate((-1, 1))]

    def edge_copy(k):
        src, dst, dx, dy = edges[k]
        return pltpu.make_async_remote_copy(
            src_ref=src, dst_ref=dst, send_sem=hs.at[k], recv_sem=hr.at[k],
            device_id=spatial(dx, dy), device_id_type=MESH)

    def leave(ks):
        for k in ks:

            @pl.when(exists(*edges[k][2:]))
            def _():
                edge_copy(k).start()

    ready = False
    for step in PLAN:
        if step[0] == "turn":
            turn(step[1])
        elif step[0] == "send":
            if not ready:
                pl.semaphore_wait(barrier, len(mates) + count(earlier))
                ready = True
            send(*step[1:])
        elif step[0] == "wait":
            arrived(*step[1:])
            if step[1][0] == 1:
                pack_ends(*step[1:])
            if step[1] != (1, 2):
                shift_z(member(*step[1]), step[2])
        elif step[0] == "ends":
            ends_so_far()
        elif step[0] == "own":
            tell(entered, earlier)
            zero = jnp.zeros((n_ch * cin, LANES), BF16)
            for c in range(3):
                X[c, 0] = zero
                X[c, cells_x + 1] = zero
            for part in range(PARTS):
                shift_z(ch, part)
        elif step[0] == "first":
            load_w.wait()
            load_b.wait()
            products(pair_of(step[1]), True, ends_x + inside)
        elif step[0] == "next":
            products(pair_of(step[1]), False, ends_x + inside)
        else:
            ends_of(far_half)
            some = count(later)

            @pl.when(some > 0)
            def _():
                pl.semaphore_wait(entered, some)

            leave(range(2))
            for part in range(PARTS):
                shift_z(member(1, 2), part)
            products(far_half, False, ends_x)
            corners()
            leave(range(4, 8))
            hx[0] = along_y(0)
            hx[1] = along_y(cells_x + 1)
            leave(range(2, 4))


    products(far_half, False, inside)
    sub = lax.broadcasted_iota(jnp.int32, (cout, cout), 0)
    across = lax.broadcasted_iota(jnp.int32, (cout, cout), 1)
    bias = jnp.sum(jnp.where(sub == across, jnp.broadcast_to(B[...], (cout, cout)), 0.0),
                   axis=1, keepdims=True)
    for x in range(cells_x):
        flat[pl.ds(x, cout, stride=cells_x), :] = along_y(x + 1) + bias

    has, has_end = (has_x[-1], has_x[1]), (has_y[-1], has_y[1])
    zeros = jnp.zeros((cout, LANES), F32)

    def take(ks):
        for k in ks:

            @pl.when(exists(-edges[k][2], -edges[k][3]))
            def _():
                edge_copy(k).wait_recv()

    for j, ks in enumerate(((1, 2, 3, 5, 7), (0, 4, 6))):
        take(ks)
        start = (0, last)[j]
        inside_y = (lane_o < CZ, lane_o >= last)[j]
        beyond = jnp.where(has_end[j], ry[1 - j], zeros)
        for x in range(cells_x):
            extra = jnp.where(inside_y, roll(beyond, start - x * CZ), 0.0)
            if x in (0, cells_x - 1):
                i = 0 if x == 0 else 1
                packed = jnp.where(has[i] & has_end[j], rc[2 * (1 - i) + 1 - j], jnp.zeros((8, LANES), F32))
                spread = jnp.concatenate([roll(packed, start - g * CZ) for g in range(groups)], axis=0)
                extra = extra + jnp.where(inside_y, spread, 0.0)
                if j == 0:
                    extra = extra + jnp.where(has[i], rx[1 - i], zeros)
            spot = pl.ds(x, cout, stride=cells_x)
            flat[spot, :] = flat[spot, :] + extra
    o_ref[...] = flat[...].reshape(cout, cells_x, LANES).astype(BF16)
    for k, (_, _, dx, dy) in enumerate(edges):

        @pl.when(exists(dx, dy))
        def _():
            edge_copy(k).wait_send()

    for copy in sent:
        copy.wait_send()


def solution(mesh):
    sizes = tuple(mesh.shape[a] for a in ("sx", "sy", "ch"))
    n_ch = sizes[2]

    def per_device(volume, weight, bias):
        cin, cells_x, merged = volume.shape
        cout = weight.shape[3]
        call = pl.pallas_call(
            lambda *refs: kernel(sizes, *refs),
            out_shape=pltpu.VMEM((cout, cells_x, merged), BF16),
            in_specs=[
                pl.BlockSpec(memory_space=pltpu.HBM),
                pl.BlockSpec(memory_space=pltpu.HBM),
                pl.BlockSpec(memory_space=pltpu.HBM),
            ],
            out_specs=pl.BlockSpec(memory_space=pltpu.VMEM),
            scratch_shapes=[
                pltpu.VMEM((3, cells_x + 2, n_ch * cin, LANES), BF16),
                pltpu.VMEM(weight.shape, BF16),
                pltpu.VMEM((cin, cells_x, LANES), BF16),
                pltpu.VMEM((1, cout), F32),
                pltpu.VMEM((cells_x + 2, 3 * cout, LANES), F32),
                pltpu.VMEM((2, 9, n_ch // 2 * cin, LANES), BF16),
                pltpu.VMEM((cout * cells_x, LANES), F32),
                pltpu.VMEM((2, cout, LANES), F32),
                pltpu.VMEM((2, cout, LANES), F32),
                pltpu.VMEM((4, 8, LANES), F32),
                pltpu.VMEM((2, cout, LANES), F32),
                pltpu.VMEM((2, cout, LANES), F32),
                pltpu.VMEM((4, 8, LANES), F32),
                pltpu.SemaphoreType.DMA((2 + PARTS,)),
                pltpu.SemaphoreType.DMA((n_ch * PARTS,)),
                pltpu.SemaphoreType.DMA((n_ch * PARTS,)),
                pltpu.SemaphoreType.DMA((8,)),
                pltpu.SemaphoreType.DMA((8,)),
                pltpu.SemaphoreType.REGULAR,
            ],
            compiler_params=pltpu.CompilerParams(
                collective_id=0, has_side_effects=True, vmem_limit_bytes=32 << 20),
            name="conv_gather",
        )
        return call(*[pltpu.with_memory_space_constraint(a, pltpu.HBM) for a in (volume, weight, bias.reshape(1, cout))])

    return jax.shard_map(
        per_device,
        mesh=mesh,
        in_specs=(P("ch", "sx", "sy"), P(None, None, None, "ch", None), P("ch")),
        out_specs=P("ch", "sx", "sy"),
        check_vma=False,
    )
```

```python
import jax
import jax.numpy as jnp
from jax import lax
from jax.experimental import pallas as pl
from jax.experimental.pallas import tpu as pltpu
from jax.sharding import PartitionSpec as P

CZ = 16
LANES = 128
MESH = pl.DeviceIdType.MESH
PARTS = 2
PLAN = [
    ('turn', 0),
    ('send', (0, 0), 0, (1, 0)),
    ('send', (0, 0), 0, (0, 2)),
    ('turn', 1),
    ('send', (0, 0), 1, (1, 0)),
    ('send', (0, 0), 1, (0, 2)),
    ('send', (0, 0), 1, (0, 1)),
    ('send', (0, 0), 0, (0, 3)),
    ('send', (0, 0), 0, (0, 1)),
    ('send', (0, 0), 1, (0, 3)),
    ('own',),
    ('wait', (1, 0), 0),
    ('send', (1, 0), 0, (0, 1)),
    ('send', (1, 0), 0, (0, 3)),
    ('wait', (0, 2), 0),
    ('send', (0, 2), 0, (1, 0)),
    ('wait', (1, 0), 1),
    ('send', (1, 0), 1, (0, 1)),
    ('send', (1, 0), 1, (0, 3)),
    ('wait', (0, 2), 1),
    ('send', (0, 2), 1, (1, 0)),
    ('wait', (0, 1), 0),
    ('wait', (0, 1), 1),
    ('first', (0, 0)),
    ('wait', (0, 3), 0),
    ('wait', (0, 3), 1),
    ('next', (0, 2)),
    ('ends',),
    ('wait', (1, 1), 0),
    ('wait', (1, 1), 1),
    ('wait', (1, 3), 0),
    ('wait', (1, 3), 1),
    ('wait', (1, 2), 0),
    ('wait', (1, 2), 1),
    ('last',),
]
F32 = jnp.float32
BF16 = jnp.bfloat16


def kernel(sizes, v_hbm, w_hbm, b_hbm, o_ref, X, W, V, B, acc, ends, flat, hx, hy, hc, rx, ry, rc,
           load_sem, gs, gr, hs, hr, entered):
    n_sx, n_sy, n_ch = sizes
    half_ch = n_ch // 2
    cin, cells_x = V.shape[0], V.shape[1]
    cout = W.shape[3]
    group = half_ch * cin
    sx, sy, ch = lax.axis_index("sx"), lax.axis_index("sy"), lax.axis_index("ch")
    h, y = ch // half_ch, lax.rem(ch, half_ch)

    def member(other, k):
        across = (y, y + 1 - 2 * lax.rem(y, 2), lax.rem(y + 2, 4), 3 - y)[k]
        return (1 - h if other else h) * half_ch + across

    def mate(other, k):
        return (sx, sy, member(other, k))

    def spatial(dx, dy):
        return (sx + dx, sy + dy, ch)

    has_x = {-1: sx > 0, 0: sx >= 0, 1: sx < n_sx - 1}
    has_y = {-1: sy > 0, 0: sy >= 0, 1: sy < n_sy - 1}

    def exists(dx, dy):
        return has_x[dx] & has_y[dy]

    step_ch = cin // PARTS
    load_v = [pltpu.make_async_copy(v_hbm.at[pl.ds(p * step_ch, step_ch)], V.at[pl.ds(p * step_ch, step_ch)],
                                    load_sem.at[2 + p]) for p in range(PARTS)]
    load_w = pltpu.make_async_copy(w_hbm, W, load_sem.at[0])
    load_b = pltpu.make_async_copy(b_hbm, B, load_sem.at[1])
    for load in load_v:
        load.start()
    load_b.start()
    load_w.start()

    barrier = pltpu.get_barrier_semaphore()
    mates = sorted({step[3] for step in PLAN if step[0] == "send"})
    later = [(0, 1), (-1, 1), (1, 1), (1, 0)]
    earlier = [(-dx, -dy) for dx, dy in later]
    for m in mates:
        pl.semaphore_signal(barrier, inc=1, device_id=mate(*m), device_id_type=MESH)

    def tell(sem, places):
        for place in places:

            @pl.when(exists(*place))
            def _():
                pl.semaphore_signal(sem, inc=1, device_id=spatial(*place), device_id_type=MESH)

    def count(places):
        return sum(jnp.where(exists(*place), 1, 0) for place in places)

    tell(barrier, later)

    lane = lax.broadcasted_iota(jnp.int32, (step_ch, LANES), 1)
    z = lax.rem(lane, CZ)

    def rows(who, part):
        return pl.ds(pl.multiple_of(who * cin + part * step_ch, step_ch), step_ch)

    def turn(part):
        load_v[part].wait()
        n = step_ch * cells_x
        flat[part * n : (part + 1) * n] = V[pl.ds(part * step_ch, step_ch)].astype(F32).reshape(n, LANES)
        for x in range(cells_x):
            piece = flat[pl.ds(part * n + x, step_ch, stride=cells_x), :]
            X[1, x + 1, rows(ch, part), :] = piece.astype(BF16)

    def shift_z(who, part):
        r = rows(who, part)
        for x in range(1, cells_x + 1):
            v = X[1, x, r, :]
            X[0, x, r, :] = jnp.where(z == 0, jnp.zeros_like(v), pltpu.roll(v, 1, 1))
            X[2, x, r, :] = jnp.where(z == CZ - 1, jnp.zeros_like(v), pltpu.roll(v, LANES - 1, 1))

    last = LANES - CZ
    along_x = lane // CZ
    valid_x = (along_x >= 1, None, along_x < cells_x - 1)
    valid_z = (z >= 1, None, z < CZ - 1)

    def roll(v, by):
        by = by % LANES
        return pltpu.roll(v, by, 1) if by else v

    def pack_ends(block, part):
        r = rows(member(*block), part)
        within = lax.rem(member(*block), half_ch) * cin + part * step_ch
        to = pl.ds(pl.multiple_of(within, step_ch), step_ch)
        for e, start in enumerate((0, last)):
            packed = jnp.zeros((step_ch, LANES), BF16)
            for x in range(cells_x):
                packed = jnp.where(along_x == x, roll(X[1, x + 1, r, :], x * CZ - start), packed)
            for a in range(3):
                for c in range(3):
                    v = roll(packed, (1 - a) * CZ + 1 - c)
                    for valid in (valid_x[a], valid_z[c]):
                        if valid is not None:
                            v = jnp.where(valid, v, jnp.zeros_like(v))
                    ends[e, 3 * a + c, to, :] = v

    def block_copy(block, part, out, slot, to):
        piece = X.at[1, 1 : cells_x + 1, rows(member(*block), part), :]
        return pltpu.make_async_remote_copy(
            src_ref=piece, dst_ref=piece, send_sem=gs.at[out], recv_sem=gr.at[slot],
            device_id=mate(*to), device_id_type=MESH)

    sent = []

    def send(block, part, to):
        other, k = block[0] ^ to[0], block[1] ^ to[1]
        copy = block_copy(block, part, len(sent), (other * half_ch + k) * PARTS + part, to)
        copy.start()
        sent.append(copy)

    def arrived(block, part):
        block_copy(block, part, 0, (block[0] * half_ch + block[1]) * PARTS + part, (1, 0)).wait_recv()

    pair = 2 * cin

    def pair_of(block):
        return pl.ds(pl.multiple_of(member(*block) // 2 * pair, pair), pair)

    ends_x = [(0,), (cells_x + 1,)]
    inside = [(x, x + 1) for x in range(1, cells_x + 1, 2)]

    def products(cols, first, spans):
        for slabs in spans:
            taps = [a for a in range(3) if any(0 < o + a - 1 < cells_x + 1 for o in slabs)]
            lhs = jnp.concatenate(
                [W[a, :, c, :, cols].reshape(3 * cout, cols.size) for a in taps for c in range(3)], axis=1)
            rhs = jnp.concatenate(
                [jnp.concatenate([X[c, o + a - 1, cols, :] for o in slabs], axis=1)
                 for a in taps for c in range(3)], axis=0)
            r = jnp.dot(lhs, rhs, preferred_element_type=F32)
            for j, o in enumerate(slabs):
                part = r[:, LANES * j : LANES * (j + 1)]
                acc[o] = part if first else acc[o] + part

    lane_o = lax.broadcasted_iota(jnp.int32, (cout, LANES), 1)

    def taps_of(s, b):
        return acc[s, b * cout : (b + 1) * cout]

    def along_y(s):
        up = jnp.where(lane_o < CZ, 0.0, pltpu.roll(taps_of(s, 0), CZ, 1))
        down = jnp.where(lane_o >= last, 0.0, pltpu.roll(taps_of(s, 2), LANES - CZ, 1))
        return taps_of(s, 1) + up + down

    groups = cout // 8
    lane_8 = lax.broadcasted_iota(jnp.int32, (8, LANES), 1)
    def corners():
        for i, s in enumerate((0, cells_x + 1)):
            for j, (b, start) in enumerate(((2, 0), (0, last))):
                corner = jnp.zeros((8, LANES), F32)
                for g in range(groups):
                    here = (lane_8 >= g * CZ) & (lane_8 < (g + 1) * CZ)
                    piece = acc[s, b * cout + 8 * g : b * cout + 8 * g + 8]
                    corner = jnp.where(here, roll(piece, g * CZ - start), corner)
                hc[2 * i + j] = corner

    def ends_so_far():
        low = jnp.zeros((cout, LANES), F32)
        high = jnp.zeros((cout, LANES), F32)
        for x in range(cells_x):
            here = (lane_o >= x * CZ) & (lane_o < (x + 1) * CZ)
            low = jnp.where(here, roll(taps_of(x + 1, 2), x * CZ), low)
            high = jnp.where(here, roll(taps_of(x + 1, 0), x * CZ - last), high)
        hy[0] = low
        hy[1] = high

    far_half = pl.ds(pl.multiple_of((1 - h) * group, group), group)

    def ends_of(cols):
        for e, b in enumerate((2, 0)):
            lhs = jnp.concatenate([W[a, b, c, :, cols] for a in range(3) for c in range(3)], axis=1)
            rhs = jnp.concatenate([ends[e, t] for t in range(9)], axis=0)
            hy[e] = hy[e] + jnp.dot(lhs, rhs, preferred_element_type=F32)

    edges = [(hy.at[0], ry.at[0], 0, -1), (hy.at[1], ry.at[1], 0, 1),
             (hx.at[0], rx.at[0], -1, 0), (hx.at[1], rx.at[1], 1, 0)]
    edges += [(hc.at[2 * i + j], rc.at[2 * i + j], dx, dy)
              for i, dx in enumerate((-1, 1)) for j, dy in enumerate((-1, 1))]

    def edge_copy(k):
        src, dst, dx, dy = edges[k]
        return pltpu.make_async_remote_copy(
            src_ref=src, dst_ref=dst, send_sem=hs.at[k], recv_sem=hr.at[k],
            device_id=spatial(dx, dy), device_id_type=MESH)

    def leave(ks):
        for k in ks:

            @pl.when(exists(*edges[k][2:]))
            def _():
                edge_copy(k).start()

    ready = False
    for step in PLAN:
        if step[0] == "turn":
            turn(step[1])
        elif step[0] == "send":
            if not ready:
                pl.semaphore_wait(barrier, len(mates) + count(earlier))
                ready = True
            send(*step[1:])
        elif step[0] == "wait":
            arrived(*step[1:])
            if step[1][0] == 1:
                pack_ends(*step[1:])
            if step[1] != (1, 2):
                shift_z(member(*step[1]), step[2])
        elif step[0] == "ends":
            ends_so_far()
        elif step[0] == "own":
            tell(entered, earlier)
            zero = jnp.zeros((n_ch * cin, LANES), BF16)
            for c in range(3):
                X[c, 0] = zero
                X[c, cells_x + 1] = zero
            for part in range(PARTS):
                shift_z(ch, part)
        elif step[0] == "first":
            load_w.wait()
            load_b.wait()
            products(pair_of(step[1]), True, ends_x + inside)
        elif step[0] == "next":
            products(pair_of(step[1]), False, ends_x + inside)
        else:
            ends_of(far_half)
            some = count(later)

            @pl.when(some > 0)
            def _():
                pl.semaphore_wait(entered, some)

            leave(range(2))
            for part in range(PARTS):
                shift_z(member(1, 2), part)
            products(far_half, False, ends_x)
            corners()
            leave(range(4, 8))
            hx[0] = along_y(0)
            hx[1] = along_y(cells_x + 1)
            leave(range(2, 4))


    products(far_half, False, inside)
    sub = lax.broadcasted_iota(jnp.int32, (cout, cout), 0)
    across = lax.broadcasted_iota(jnp.int32, (cout, cout), 1)
    bias = jnp.sum(jnp.where(sub == across, jnp.broadcast_to(B[...], (cout, cout)), 0.0),
                   axis=1, keepdims=True)
    for x in range(cells_x):
        flat[pl.ds(x, cout, stride=cells_x), :] = along_y(x + 1) + bias

    has, has_end = (has_x[-1], has_x[1]), (has_y[-1], has_y[1])
    zeros = jnp.zeros((cout, LANES), F32)

    def take(ks):
        for k in ks:

            @pl.when(exists(-edges[k][2], -edges[k][3]))
            def _():
                edge_copy(k).wait_recv()

    for j, ks in enumerate(((1, 2, 3, 5, 7), (0, 4, 6))):
        take(ks)
        start = (0, last)[j]
        inside_y = (lane_o < CZ, lane_o >= last)[j]
        beyond = jnp.where(has_end[j], ry[1 - j], zeros)
        for x in range(cells_x):
            extra = jnp.where(inside_y, roll(beyond, start - x * CZ), 0.0)
            if x in (0, cells_x - 1):
                i = 0 if x == 0 else 1
                packed = jnp.where(has[i] & has_end[j], rc[2 * (1 - i) + 1 - j], jnp.zeros((8, LANES), F32))
                spread = jnp.concatenate([roll(packed, start - g * CZ) for g in range(groups)], axis=0)
                extra = extra + jnp.where(inside_y, spread, 0.0)
                if j == 0:
                    extra = extra + jnp.where(has[i], rx[1 - i], zeros)
            spot = pl.ds(x, cout, stride=cells_x)
            flat[spot, :] = flat[spot, :] + extra
    o_ref[...] = flat[...].reshape(cout, cells_x, LANES).astype(BF16)
    for k, (_, _, dx, dy) in enumerate(edges):

        @pl.when(exists(dx, dy))
        def _():
            edge_copy(k).wait_send()

    for copy in sent:
        copy.wait_send()


def solution(mesh):
    sizes = tuple(mesh.shape[a] for a in ("sx", "sy", "ch"))
    n_ch = sizes[2]

    def per_device(volume, weight, bias):
        cin, cells_x, merged = volume.shape
        cout = weight.shape[3]
        call = pl.pallas_call(
            lambda *refs: kernel(sizes, *refs),
            out_shape=pltpu.VMEM((cout, cells_x, merged), BF16),
            in_specs=[
                pl.BlockSpec(memory_space=pltpu.HBM),
                pl.BlockSpec(memory_space=pltpu.HBM),
                pl.BlockSpec(memory_space=pltpu.HBM),
            ],
            out_specs=pl.BlockSpec(memory_space=pltpu.VMEM),
            scratch_shapes=[
                pltpu.VMEM((3, cells_x + 2, n_ch * cin, LANES), BF16),
                pltpu.VMEM(weight.shape, BF16),
                pltpu.VMEM((cin, cells_x, LANES), BF16),
                pltpu.VMEM((1, cout), F32),
                pltpu.VMEM((cells_x + 2, 3 * cout, LANES), F32),
                pltpu.VMEM((2, 9, n_ch // 2 * cin, LANES), BF16),
                pltpu.VMEM((cout * cells_x, LANES), F32),
                pltpu.VMEM((2, cout, LANES), F32),
                pltpu.VMEM((2, cout, LANES), F32),
                pltpu.VMEM((4, 8, LANES), F32),
                pltpu.VMEM((2, cout, LANES), F32),
                pltpu.VMEM((2, cout, LANES), F32),
                pltpu.VMEM((4, 8, LANES), F32),
                pltpu.SemaphoreType.DMA((2 + PARTS,)),
                pltpu.SemaphoreType.DMA((n_ch * PARTS,)),
                pltpu.SemaphoreType.DMA((n_ch * PARTS,)),
                pltpu.SemaphoreType.DMA((8,)),
                pltpu.SemaphoreType.DMA((8,)),
                pltpu.SemaphoreType.REGULAR,
            ],
            compiler_params=pltpu.CompilerParams(
                collective_id=0, has_side_effects=True, vmem_limit_bytes=32 << 20),
            name="conv_gather",
        )
        return call(*[pltpu.with_memory_space_constraint(a, pltpu.HBM) for a in (volume, weight, bias.reshape(1, cout))])

    return jax.shard_map(
        per_device,
        mesh=mesh,
        in_specs=(P("ch", "sx", "sy"), P(None, None, None, "ch", None), P("ch")),
        out_specs=P("ch", "sx", "sy"),
        check_vma=False,
    )
```
